32 devices in a mesh: dp: 16 (over z, y, core), shard: 2 (over x).
Axes of the slice: x: 2, y: 2, z: 4, core: 2. Of those that a mesh axis runs over, the one named last changes fastest.
Arguments:
- hidden_in: bfloat16 [8192, 768], P(('dp', 'shard')), may hold values from -6 to 6
- cotangent: bfloat16 [8192, 768], P(('dp', 'shard')), may hold values from -6 to 6
- segment_ids: int32 [8192], P(('dp', 'shard')), may hold values from 0 to 7, as said below
- live_mask: int32 [8192], P(('dp', 'shard')), may hold values from 0 to 1, as said below
- attend_gain: bfloat16 [768], P('shard'), may hold values from 0.5 to 1.5
- attend_shift: bfloat16 [768], P('shard'), may hold values from -3 to 3
- feed_gain: bfloat16 [768], P('shard'), may hold values from 0.5 to 1.5
- feed_shift: bfloat16 [768], P('shard'), may hold values from -3 to 3
- triple_weight: bfloat16 [768, 2304], P('shard')
- triple_bias: bfloat16 [2304], P('shard'), may hold values from -3 to 3
- output_weight: bfloat16 [768, 768], P('shard'), may hold values from -0.875 to 0.875
- output_bias: bfloat16 [768], P('shard'), may hold values from -3 to 3
- expand_weight: bfloat16 [768, 3072], P(None, 'shard'), may hold values from -0.21875 to 0.21875
- expand_bias: bfloat16 [3072], P('shard'), may hold values from -3 to 3
- reduce_weight: bfloat16 [3072, 768], P('shard'), may hold values from -0.109375 to 0.109375
- reduce_bias: bfloat16 [768], P('shard'), may hold values from -3 to 3
Outputs:
- block_out: bfloat16 [8192, 768], P(('dp', 'shard'))
- input_slope: float32 [8192, 768], P(('dp', 'shard'))
- attend_gain_gradient: float32 [768], P('shard')
- attend_shift_gradient: float32 [768], P('shard')
- feed_gain_gradient: float32 [768], P('shard')
- feed_shift_gradient: float32 [768], P('shard')
- triple_weight_gradient: float32 [768, 2304], P('shard')
- triple_bias_gradient: float32 [2304], P('shard')
- output_weight_gradient: float32 [768, 768], P('shard')
- output_bias_gradient: float32 [768], P('shard')
- expand_weight_gradient: float32 [768, 3072], P(None, 'shard')
- expand_bias_gradient: float32 [3072], P('shard')
- reduce_weight_gradient: float32 [3072, 768], P('shard')
- reduce_bias_gradient: float32 [768], P('shard')
The draws below stay inside these ranges and needn't reach their ends.
Inputs may be any that keep to these rules, and one draw needn't show every extreme that they name: `segment_ids`: ids start at 0 in each device's 256 slots and never fall along them; slots of one device with one id form one sequence; a device holds at most 8 sequences, some device exactly 8. `live_mask`: in each device's 256 slots the live ones come first, at least 64 of them.
All inputs are finite; a program needn't handle non-finite values.
Results may differ from the reference program's by a relative error of at most 0.017.
Values may be sent and summed in bfloat16 or wider, within the bound.
No kernel may reach another device: no remote copies, remote signals or barrier semaphores. Data moves between devices by JAX's collectives and lax.ppermute only.
A program may use at most 128 MiB of HBM per device.

```python
import math
import jax
import jax.numpy as jnp
from jax import lax

D = 768
HEADS = 12
HEAD = 64
FF = 3072
ROT = 16
TOK_DEV = 256
TOKENS = 8192


def layout(key):
    rows = TOKENS // TOK_DEV
    counts = jax.random.randint(jax.random.fold_in(key, 31), (rows,), TOK_DEV // 4, TOK_DEV + 1)
    fullrow = jax.random.randint(jax.random.fold_in(key, 32), (), 0, rows)
    counts = jnp.where(jnp.arange(rows) == fullrow, TOK_DEV, counts)
    place = jnp.arange(TOK_DEV)
    live = (place[None, :] < counts[:, None]).astype(jnp.int32)
    cuts = jax.random.randint(jax.random.fold_in(key, 33), (rows,), 0, 8)
    cuts = jnp.where(jnp.arange(rows) == fullrow, 7, cuts)
    row_keys = jax.random.split(jax.random.fold_in(key, 34), rows)
    orders = jax.vmap(lambda k: jax.random.permutation(k, TOK_DEV - 1))(row_keys)
    ranks = jnp.argsort(orders, axis=1).astype(jnp.int32)
    inner = (ranks < cuts[:, None]).astype(jnp.int32)
    breaks = jnp.concatenate([jnp.zeros((rows, 1), jnp.int32), inner], axis=1)
    segment = jnp.cumsum(breaks, axis=1).astype(jnp.int32)
    return (segment.reshape(TOKENS), live.reshape(TOKENS))


def draw_segment_ids(key, part):
    return layout(key)[0]


def draw_live_mask(key, part):
    return layout(key)[1]


def draw_triple_weight(key, part):
    base = jax.random.normal(jax.random.fold_in(key, 21), (D, 3 * D), jnp.float32) / math.sqrt(D)
    return base.astype(jnp.bfloat16)


def block_scale(rng, dims, cuts, least, largest):
    def one(axis_at, shards_of):
        draws = jax.random.uniform(jax.random.fold_in(jax.random.fold_in(rng, 6), axis_at), (shards_of,), jnp.float32, least / len(cuts), largest / len(cuts))
        return jnp.repeat(jnp.exp(draws), dims[axis_at] // shards_of).reshape((-1,) + (1,) * (len(dims) - axis_at - 1))

    factor_of = one(*cuts[0])
    for cut in cuts[1:]:
        factor_of = factor_of * one(*cut)
    return factor_of


def scatter_about(rng, dims, scale, most, shards=(), dtype=jnp.bfloat16):
    loudness = block_scale(rng, dims, shards, -0.22, 0.18) if shards else 1.0
    values = jax.random.normal(rng, dims, jnp.float32) * scale * loudness
    return jnp.minimum(jnp.maximum(values, -most), most).astype(dtype)


def setup_inputs(seed: int = 0) -> dict:
    arg_keys = jax.random.split(jax.random.key(seed), 17)
    return {
        "hidden_in": scatter_about(arg_keys[0], (TOKENS, D), 1.0, 6.0, ((0, 32),)),
        "cotangent": scatter_about(arg_keys[1], (TOKENS, D), 1.0, 6.0, ((0, 32),)),
        "segment_ids": draw_segment_ids(jax.random.fold_in(arg_keys[16], 71), 0),
        "live_mask": draw_live_mask(jax.random.fold_in(arg_keys[16], 71), 0),
        "attend_gain": jnp.clip(1.0 + 0.1 * jax.random.normal(arg_keys[4], (D,), jnp.float32), 0.5, 1.5).astype(jnp.bfloat16),
        "attend_shift": scatter_about(arg_keys[5], (D,), 0.5, 3.0, ((0, 2),)),
        "feed_gain": jnp.clip(1.0 + 0.1 * jax.random.normal(arg_keys[6], (D,), jnp.float32), 0.5, 1.5).astype(jnp.bfloat16),
        "feed_shift": scatter_about(arg_keys[7], (D,), 0.5, 3.0, ((0, 2),)),
        "triple_weight": draw_triple_weight(jax.random.fold_in(arg_keys[16], 71), 0),
        "triple_bias": scatter_about(arg_keys[9], (3 * D,), 0.5, 3.0, ((0, 2),)),
        "output_weight": scatter_about(arg_keys[10], (D, D), (D // 16) ** -0.5, 0.875, ((0, 2),)),
        "output_bias": scatter_about(arg_keys[11], (D,), 0.5, 3.0, ((0, 2),)),
        "expand_weight": scatter_about(arg_keys[12], (D, FF), D ** -0.5, 0.21875, ((1, 2),)),
        "expand_bias": scatter_about(arg_keys[13], (FF,), 0.5, 3.0, ((0, 2),)),
        "reduce_weight": scatter_about(arg_keys[14], (FF, D), FF ** -0.5, 0.109375, ((0, 2),)),
        "reduce_bias": scatter_about(arg_keys[15], (D,), 0.5, 3.0, ((0, 2),)),
    }


EPSILON = 1e-05
ROOT_HALF = 0.7071067811865476
DENSITY = 0.3989422804014327
NEGATIVE = -1e+30

def normalize(values):
    mean = lax.optimization_barrier(jnp.mean(values, axis=-1, keepdims=True))
    centered = values - mean
    spread = lax.optimization_barrier(jnp.mean(centered * centered, axis=-1, keepdims=True))
    scale = lax.rsqrt(spread + EPSILON)
    return (centered * scale, scale)

def norm_back(grad_out, normed, scale, gain):
    scaled = grad_out * gain
    first = lax.optimization_barrier(jnp.mean(scaled, axis=-1, keepdims=True))
    second = lax.optimization_barrier(jnp.mean(scaled * normed, axis=-1, keepdims=True))
    return scale * (scaled - first - normed * second)

def smooth_gate(values):
    return 0.5 * values * (1.0 + lax.erf(values * ROOT_HALF))

def smooth_slope(values):
    return 0.5 * (1.0 + lax.erf(values * ROOT_HALF)) + values * DENSITY * jnp.exp(-0.5 * values * values)

def rotary_tables(segment_row):
    count = segment_row.shape[0]
    index = jnp.arange(count)
    same = segment_row[:, None] == segment_row[None, :]
    before = index[None, :] < index[:, None]
    position = lax.optimization_barrier(jnp.sum((same & before).astype(jnp.float32), axis=1))
    freqs = jnp.power(10000.0, -jnp.arange(0, ROT, 2).astype(jnp.float32) / ROT)
    angle = position[:, None] * freqs[None, :]
    angle = jnp.concatenate([angle, angle], axis=1)
    return (jnp.cos(angle), jnp.sin(angle))

def allowed_mask(segment_row, live_row):
    count = segment_row.shape[0]
    index = jnp.arange(count)
    same = segment_row[:, None] == segment_row[None, :]
    causal = index[None, :] <= index[:, None]
    both = (live_row[:, None] > 0) & (live_row[None, :] > 0)
    diagonal = index[:, None] == index[None, :]
    return same & causal & (both | diagonal)

def rotate(heads, cosine, sine):
    half = ROT // 2
    part = heads[..., :ROT]
    turned = jnp.concatenate([-part[..., half:], part[..., :half]], axis=-1)
    mixed = part * jnp.expand_dims(cosine, -2) + turned * jnp.expand_dims(sine, -2)
    return jnp.concatenate([mixed, heads[..., ROT:]], axis=-1)

def rotate_back(grads, cosine, sine):
    half = ROT // 2
    part = grads[..., :ROT]
    sined = part * jnp.expand_dims(sine, -2)
    turned = jnp.concatenate([sined[..., half:], -sined[..., :half]], axis=-1)
    mixed = part * jnp.expand_dims(cosine, -2) + turned
    return jnp.concatenate([mixed, grads[..., ROT:]], axis=-1)

def attend(query, keys, values, allowed):
    scale = 1.0 / math.sqrt(HEAD)
    scores = jnp.einsum('qhd,khd->hqk', query.astype(jnp.float32), keys.astype(jnp.float32)) * scale
    scores = jnp.where(allowed[None], scores, NEGATIVE)
    top = lax.optimization_barrier(jnp.max(scores, axis=-1, keepdims=True))
    total = lax.optimization_barrier(jnp.sum(jnp.exp(scores - top), axis=-1, keepdims=True))
    logsum = top + jnp.log(total)
    probs = jnp.exp(scores - logsum).astype(jnp.bfloat16)
    context = jnp.einsum('hqk,khd->qhd', probs.astype(jnp.float32), values.astype(jnp.float32))
    return (context.astype(jnp.bfloat16), logsum)

def attend_back(query, keys, values, allowed, logsum, context_grad):
    scale = 1.0 / math.sqrt(HEAD)
    query32 = query.astype(jnp.float32)
    keys32 = keys.astype(jnp.float32)
    scores = jnp.einsum('qhd,khd->hqk', query32, keys32) * scale
    scores = jnp.where(allowed[None], scores, NEGATIVE)
    probs = jnp.exp(scores - logsum)
    probs_bf = probs.astype(jnp.bfloat16)
    grad32 = context_grad.astype(jnp.float32)
    value_grad = jnp.einsum('hqk,qhd->khd', probs_bf.astype(jnp.float32), grad32)
    prob_grad = jnp.einsum('qhd,khd->hqk', grad32, values.astype(jnp.float32))
    delta = lax.optimization_barrier(jnp.sum(probs * prob_grad, axis=-1, keepdims=True))
    score_grad = (probs * (prob_grad - delta) * scale).astype(jnp.bfloat16).astype(jnp.float32)
    query_grad = jnp.einsum('hqk,khd->qhd', score_grad, keys32)
    key_grad = jnp.einsum('hqk,qhd->khd', score_grad, query32)
    return (query_grad, key_grad, value_grad)

def product(left, right):
    return jnp.dot(left, right, preferred_element_type=jnp.float32)

def reference(hidden_in, cotangent, segment_ids, live_mask, attend_gain, attend_shift, feed_gain, feed_shift, triple_weight, triple_bias, output_weight, output_bias, expand_weight, expand_bias, reduce_weight, reduce_bias):
    rows = TOKENS // TOK_DEV
    group = math.gcd(rows, 16)
    turns = rows // group
    width = HEADS * HEAD
    block = group * TOK_DEV
    x_blocks = hidden_in.reshape(turns, block, width)
    c_blocks = cotangent.reshape(turns, block, width)
    s_blocks = segment_ids.reshape(turns, group, TOK_DEV)
    l_blocks = live_mask.reshape(turns, group, TOK_DEV)
    gain_one = attend_gain.astype(jnp.float32)
    shift_one = attend_shift.astype(jnp.float32)
    gain_two = feed_gain.astype(jnp.float32)
    shift_two = feed_shift.astype(jnp.float32)

    def one_block(totals, inputs):
        x_block, c_block, s_block, l_block = inputs
        inputs32 = x_block.astype(jnp.float32)
        normed, scale = normalize(inputs32)
        act_one = (normed * gain_one + shift_one).astype(jnp.bfloat16)
        act_two = (normed * gain_two + shift_two).astype(jnp.bfloat16)
        cosine, sine = jax.vmap(rotary_tables)(s_block)
        allowed = jax.vmap(allowed_mask)(s_block, l_block)
        triple = product(act_one, triple_weight) + triple_bias.astype(jnp.float32)
        shaped = (group, TOK_DEV, HEADS, HEAD)
        query = rotate(triple[:, :width].reshape(shaped), cosine, sine).astype(jnp.bfloat16)
        keys = rotate(triple[:, width:2 * width].reshape(shaped), cosine, sine).astype(jnp.bfloat16)
        values = triple[:, 2 * width:].reshape(shaped).astype(jnp.bfloat16)
        context, logsum = jax.vmap(attend)(query, keys, values, allowed)
        context_flat = context.reshape(block, width)
        attention = product(context_flat, output_weight) + output_bias.astype(jnp.float32)
        feed_pre = product(act_two, expand_weight) + expand_bias.astype(jnp.float32)
        feed_hidden = smooth_gate(feed_pre).astype(jnp.bfloat16)
        feed = product(feed_hidden, reduce_weight)
        block_out = (inputs32 + attention + feed + reduce_bias.astype(jnp.float32)).astype(jnp.bfloat16)
        upstream = c_block.astype(jnp.float32) * l_block.reshape(block).astype(jnp.float32)[:, None]
        upstream_bf = upstream.astype(jnp.bfloat16)
        bias_term = lax.optimization_barrier(jnp.sum(upstream, axis=0))
        reduce_term = product(feed_hidden.T, upstream_bf)
        pre_grad = product(upstream_bf, reduce_weight.T) * smooth_slope(feed_pre)
        pre_grad_bf = pre_grad.astype(jnp.bfloat16)
        expand_bias_term = lax.optimization_barrier(jnp.sum(pre_grad, axis=0))
        expand_term = product(act_two.T, pre_grad_bf)
        feed_input_grad = product(pre_grad_bf, expand_weight.T)
        output_term = product(context_flat.T, upstream_bf)
        context_grad = product(upstream_bf, output_weight.T).astype(jnp.bfloat16).reshape(shaped)
        query_grad, key_grad, value_grad = jax.vmap(attend_back)(query, keys, values, allowed, logsum, context_grad)
        triple_grad = jnp.concatenate([rotate_back(query_grad, cosine, sine).reshape(block, width), rotate_back(key_grad, cosine, sine).reshape(block, width), value_grad.reshape(block, width)], axis=1)
        triple_bias_term = lax.optimization_barrier(jnp.sum(triple_grad, axis=0))
        triple_grad_bf = triple_grad.astype(jnp.bfloat16)
        triple_term = product(act_one.T, triple_grad_bf)
        attend_input_grad = product(triple_grad_bf, triple_weight.T)
        gain_one_term = lax.optimization_barrier(jnp.sum(attend_input_grad * normed, axis=0))
        shift_one_term = lax.optimization_barrier(jnp.sum(attend_input_grad, axis=0))
        gain_two_term = lax.optimization_barrier(jnp.sum(feed_input_grad * normed, axis=0))
        shift_two_term = lax.optimization_barrier(jnp.sum(feed_input_grad, axis=0))
        input_slope = upstream + norm_back(attend_input_grad, normed, scale, gain_one) + norm_back(feed_input_grad, normed, scale, gain_two)
        terms = (gain_one_term, shift_one_term, gain_two_term, shift_two_term, triple_term, triple_bias_term, output_term, bias_term, expand_term, expand_bias_term, reduce_term)
        new_totals = tuple((a + b for a, b in zip(totals, terms)))
        return (new_totals, (block_out, input_slope))
    init = (jnp.zeros((D,), jnp.float32), jnp.zeros((D,), jnp.float32), jnp.zeros((D,), jnp.float32), jnp.zeros((D,), jnp.float32), jnp.zeros((D, 3 * D), jnp.float32), jnp.zeros((3 * D,), jnp.float32), jnp.zeros((D, D), jnp.float32), jnp.zeros((D,), jnp.float32), jnp.zeros((D, FF), jnp.float32), jnp.zeros((FF,), jnp.float32), jnp.zeros((FF, D), jnp.float32))
    totals, (outs, slopes) = lax.scan(one_block, init, (x_blocks, c_blocks, s_blocks, l_blocks))
    block_out = outs.reshape(TOKENS, D)
    input_slope = slopes.reshape(TOKENS, D)
    return (block_out, input_slope, totals[0], totals[1], totals[2], totals[3], totals[4], totals[5], totals[6], totals[7], totals[8], totals[9], totals[10], totals[7])
```

```python
import math

import jax
import jax.numpy as jnp
from jax import lax
from jax.sharding import PartitionSpec as P

HEADS = 12
HEAD = 64
ROT = 16


EPSILON = 1e-05
ROOT_HALF = 0.7071067811865476
DENSITY = 0.3989422804014327
NEGATIVE = -1e30


def product(left, right):
    return jnp.dot(left, right, preferred_element_type=jnp.float32)


def times_transposed(left, right):
    return lax.dot_general(
        left, right, (((1,), (1,)), ((), ())), preferred_element_type=jnp.float32
    )


def transposed_times(left, right):
    return lax.dot_general(
        left, right, (((0,), (0,)), ((), ())), preferred_element_type=jnp.float32
    )


def normalize(values):
    mean = jnp.mean(values, axis=-1, keepdims=True)
    centered = values - mean
    spread = jnp.mean(centered * centered, axis=-1, keepdims=True)
    scale = lax.rsqrt(spread + EPSILON)
    return (centered * scale, scale)


def norm_back(grad_out, normed, scale, gain):
    scaled = grad_out * gain
    first = jnp.mean(scaled, axis=-1, keepdims=True)
    second = jnp.mean(scaled * normed, axis=-1, keepdims=True)
    return scale * (scaled - first - normed * second)


def smooth_gate(values):
    return 0.5 * values * (1.0 + lax.erf(values * ROOT_HALF))


def smooth_slope(values):
    return 0.5 * (1.0 + lax.erf(values * ROOT_HALF)) + values * DENSITY * jnp.exp(
        -0.5 * values * values
    )


def rotary_tables(segment_row):
    count = segment_row.shape[0]
    index = jnp.arange(count)
    same = segment_row[:, None] == segment_row[None, :]
    before = index[None, :] < index[:, None]
    position = jnp.sum((same & before).astype(jnp.float32), axis=1)
    freqs = jnp.power(10000.0, -jnp.arange(0, ROT, 2).astype(jnp.float32) / ROT)
    angle = position[:, None] * freqs[None, :]
    angle = jnp.concatenate([angle, angle], axis=1)
    return (jnp.cos(angle), jnp.sin(angle))


def allowed_mask(segment_row, live_row):
    count = segment_row.shape[0]
    index = jnp.arange(count)
    same = segment_row[:, None] == segment_row[None, :]
    causal = index[None, :] <= index[:, None]
    both = (live_row[:, None] > 0) & (live_row[None, :] > 0)
    diagonal = index[:, None] == index[None, :]
    return same & causal & (both | diagonal)


def rotate(heads, cosine, sine):
    half = ROT // 2
    part = heads[..., :ROT]
    turned = jnp.concatenate([-part[..., half:], part[..., :half]], axis=-1)
    mixed = part * jnp.expand_dims(cosine, -2) + turned * jnp.expand_dims(sine, -2)
    return jnp.concatenate([mixed, heads[..., ROT:]], axis=-1)


def rotate_back(grads, cosine, sine):
    half = ROT // 2
    part = grads[..., :ROT]
    sined = part * jnp.expand_dims(sine, -2)
    turned = jnp.concatenate([sined[..., half:], -sined[..., :half]], axis=-1)
    mixed = part * jnp.expand_dims(cosine, -2) + turned
    return jnp.concatenate([mixed, grads[..., ROT:]], axis=-1)


def masked_scores(query, keys, allowed):
    scale = 1.0 / math.sqrt(HEAD)
    scores = jnp.einsum("qhd,khd->hqk", query, keys, preferred_element_type=jnp.float32) * scale
    return jnp.where(allowed[None], scores, NEGATIVE)


def attend(query, keys, values, allowed):
    scores = masked_scores(query, keys, allowed)
    top = jnp.max(scores, axis=-1, keepdims=True)
    total = jnp.sum(jnp.exp(scores - top), axis=-1, keepdims=True)
    logsum = top + jnp.log(total)
    probs = jnp.exp(scores - logsum).astype(jnp.bfloat16)
    context = jnp.einsum("hqk,khd->qhd", probs, values, preferred_element_type=jnp.float32)
    return (context.astype(jnp.bfloat16), logsum)


def attend_back(query, keys, values, allowed, logsum, context_grad):
    scale = 1.0 / math.sqrt(HEAD)
    probs = jnp.exp(masked_scores(query, keys, allowed) - logsum)
    probs_bf = probs.astype(jnp.bfloat16)
    value_grad = jnp.einsum(
        "hqk,qhd->khd", probs_bf, context_grad, preferred_element_type=jnp.float32
    )
    prob_grad = jnp.einsum("qhd,khd->hqk", context_grad, values, preferred_element_type=jnp.float32)
    delta = jnp.sum(probs * prob_grad, axis=-1, keepdims=True)
    score_grad = (probs * (prob_grad - delta) * scale).astype(jnp.bfloat16)
    query_grad = jnp.einsum("hqk,khd->qhd", score_grad, keys, preferred_element_type=jnp.float32)
    key_grad = jnp.einsum("hqk,qhd->khd", score_grad, query, preferred_element_type=jnp.float32)
    return (query_grad, key_grad, value_grad)


def gathered_body(
    hidden_in,
    cotangent,
    segment_ids,
    live_mask,
    attend_gain,
    attend_shift,
    feed_gain,
    feed_shift,
    triple_weight,
    triple_bias,
    output_weight,
    output_bias,
    expand_weight,
    expand_bias,
    reduce_weight,
    reduce_bias,
):
    tokens = hidden_in.shape[0]
    width = HEADS * HEAD
    shaped = (tokens, HEADS, HEAD)
    (
        gain_one,
        shift_one,
        gain_two,
        shift_two,
        triple_full,
        triple_bias_full,
        output_full,
        output_bias_full,
        reduce_bias_full,
    ) = (
        lax.all_gather(attend_gain, "shard", axis=0, tiled=True),
        lax.all_gather(attend_shift, "shard", axis=0, tiled=True),
        lax.all_gather(feed_gain, "shard", axis=0, tiled=True),
        lax.all_gather(feed_shift, "shard", axis=0, tiled=True),
        lax.all_gather(triple_weight, "shard", axis=0, tiled=True),
        lax.all_gather(triple_bias, "shard", axis=0, tiled=True),
        lax.all_gather(output_weight, "shard", axis=0, tiled=True),
        lax.all_gather(output_bias, "shard", axis=0, tiled=True),
        lax.all_gather(reduce_bias, "shard", axis=0, tiled=True),
    )
    inputs32 = hidden_in.astype(jnp.float32)
    normed, scale = normalize(inputs32)
    act_one = (normed * gain_one.astype(jnp.float32) + shift_one.astype(jnp.float32)).astype(
        jnp.bfloat16
    )
    act_two = (normed * gain_two.astype(jnp.float32) + shift_two.astype(jnp.float32)).astype(
        jnp.bfloat16
    )
    cosine, sine = rotary_tables(segment_ids)
    allowed = allowed_mask(segment_ids, live_mask)
    triple = product(act_one, triple_full) + triple_bias_full.astype(jnp.float32)
    query = rotate(triple[:, :width].reshape(shaped), cosine, sine).astype(jnp.bfloat16)
    keys = rotate(triple[:, width : 2 * width].reshape(shaped), cosine, sine).astype(jnp.bfloat16)
    values = triple[:, 2 * width :].reshape(shaped).astype(jnp.bfloat16)
    context, logsum = attend(query, keys, values, allowed)
    context_flat = context.reshape(tokens, width)
    attention = product(context_flat, output_full) + output_bias_full.astype(jnp.float32)
    expand_full, expand_bias_full, reduce_full = (
        lax.all_gather(expand_weight, "shard", axis=1, tiled=True),
        lax.all_gather(expand_bias, "shard", axis=0, tiled=True),
        lax.all_gather(reduce_weight, "shard", axis=0, tiled=True),
    )
    feed_pre = product(act_two, expand_full) + expand_bias_full.astype(jnp.float32)
    feed_hidden = smooth_gate(feed_pre).astype(jnp.bfloat16)
    feed = product(feed_hidden, reduce_full)
    block_out = (inputs32 + attention + feed + reduce_bias_full.astype(jnp.float32)).astype(
        jnp.bfloat16
    )
    upstream = cotangent.astype(jnp.float32) * live_mask.astype(jnp.float32)[:, None]
    upstream_bf = upstream.astype(jnp.bfloat16)
    gain_one_again, gain_two_again, triple_again, output_again = (
        lax.all_gather(attend_gain, "shard", axis=0, tiled=True),
        lax.all_gather(feed_gain, "shard", axis=0, tiled=True),
        lax.all_gather(triple_weight, "shard", axis=0, tiled=True),
        lax.all_gather(output_weight, "shard", axis=0, tiled=True),
    )
    expand_again, reduce_again = (
        lax.all_gather(expand_weight, "shard", axis=1, tiled=True),
        lax.all_gather(reduce_weight, "shard", axis=0, tiled=True),
    )
    pre_grad = times_transposed(upstream_bf, reduce_again) * smooth_slope(feed_pre)
    pre_grad_bf = pre_grad.astype(jnp.bfloat16)
    feed_input_grad = times_transposed(pre_grad_bf, expand_again)
    expand_term, expand_bias_term, reduce_term = (
        lax.psum_scatter(
            transposed_times(act_two, pre_grad_bf).astype(jnp.bfloat16),
            "shard",
            scatter_dimension=1,
            tiled=True,
        ).astype(jnp.float32),
        lax.psum_scatter(
            jnp.sum(pre_grad, axis=0).astype(jnp.bfloat16), "shard", scatter_dimension=0, tiled=True
        ).astype(jnp.float32),
        lax.psum_scatter(
            transposed_times(feed_hidden, upstream_bf).astype(jnp.bfloat16),
            "shard",
            scatter_dimension=0,
            tiled=True,
        ).astype(jnp.float32),
    )
    bias_term = jnp.sum(upstream, axis=0)
    output_term = transposed_times(context_flat, upstream_bf)
    context_grad = times_transposed(upstream_bf, output_again).astype(jnp.bfloat16).reshape(shaped)
    query_grad, key_grad, value_grad = attend_back(
        query, keys, values, allowed, logsum, context_grad
    )
    triple_grad = jnp.concatenate(
        [
            rotate_back(query_grad, cosine, sine).reshape(tokens, width),
            rotate_back(key_grad, cosine, sine).reshape(tokens, width),
            value_grad.reshape(tokens, width),
        ],
        axis=1,
    )
    triple_bias_term = jnp.sum(triple_grad, axis=0)
    triple_grad_bf = triple_grad.astype(jnp.bfloat16)
    triple_term = transposed_times(act_one, triple_grad_bf)
    attend_input_grad = times_transposed(triple_grad_bf, triple_again)
    gain_one_term = jnp.sum(attend_input_grad * normed, axis=0)
    shift_one_term = jnp.sum(attend_input_grad, axis=0)
    gain_two_term = jnp.sum(feed_input_grad * normed, axis=0)
    shift_two_term = jnp.sum(feed_input_grad, axis=0)
    input_slope = (
        upstream
        + norm_back(attend_input_grad, normed, scale, gain_one_again.astype(jnp.float32))
        + norm_back(feed_input_grad, normed, scale, gain_two_again.astype(jnp.float32))
    )
    (
        gain_one_part,
        shift_one_part,
        gain_two_part,
        shift_two_part,
        triple_part,
        triple_bias_part,
        output_part,
        bias_part,
    ) = (
        lax.psum_scatter(
            gain_one_term.astype(jnp.bfloat16), "shard", scatter_dimension=0, tiled=True
        ).astype(jnp.float32),
        lax.psum_scatter(
            shift_one_term.astype(jnp.bfloat16), "shard", scatter_dimension=0, tiled=True
        ).astype(jnp.float32),
        lax.psum_scatter(
            gain_two_term.astype(jnp.bfloat16), "shard", scatter_dimension=0, tiled=True
        ).astype(jnp.float32),
        lax.psum_scatter(
            shift_two_term.astype(jnp.bfloat16), "shard", scatter_dimension=0, tiled=True
        ).astype(jnp.float32),
        lax.psum_scatter(
            triple_term.astype(jnp.bfloat16), "shard", scatter_dimension=0, tiled=True
        ).astype(jnp.float32),
        lax.psum_scatter(
            triple_bias_term.astype(jnp.bfloat16), "shard", scatter_dimension=0, tiled=True
        ).astype(jnp.float32),
        lax.psum_scatter(
            output_term.astype(jnp.bfloat16), "shard", scatter_dimension=0, tiled=True
        ).astype(jnp.float32),
        lax.psum_scatter(
            bias_term.astype(jnp.bfloat16), "shard", scatter_dimension=0, tiled=True
        ).astype(jnp.float32),
    )
    (
        gain_one_sum,
        shift_one_sum,
        gain_two_sum,
        shift_two_sum,
        triple_sum,
        triple_bias_sum,
        output_sum,
        bias_sum,
        expand_sum,
        expand_bias_sum,
        reduce_sum,
    ) = (
        lax.psum(gain_one_part.astype(jnp.bfloat16), "dp").astype(jnp.float32),
        lax.psum(shift_one_part.astype(jnp.bfloat16), "dp").astype(jnp.float32),
        lax.psum(gain_two_part.astype(jnp.bfloat16), "dp").astype(jnp.float32),
        lax.psum(shift_two_part.astype(jnp.bfloat16), "dp").astype(jnp.float32),
        lax.psum(triple_part.astype(jnp.bfloat16), "dp").astype(jnp.float32),
        lax.psum(triple_bias_part.astype(jnp.bfloat16), "dp").astype(jnp.float32),
        lax.psum(output_part.astype(jnp.bfloat16), "dp").astype(jnp.float32),
        lax.psum(bias_part.astype(jnp.bfloat16), "dp").astype(jnp.float32),
        lax.psum(expand_term.astype(jnp.bfloat16), "dp").astype(jnp.float32),
        lax.psum(expand_bias_term.astype(jnp.bfloat16), "dp").astype(jnp.float32),
        lax.psum(reduce_term.astype(jnp.bfloat16), "dp").astype(jnp.float32),
    )
    return (
        block_out,
        input_slope,
        gain_one_sum,
        shift_one_sum,
        gain_two_sum,
        shift_two_sum,
        triple_sum,
        triple_bias_sum,
        output_sum,
        bias_sum,
        expand_sum,
        expand_bias_sum,
        reduce_sum,
        bias_sum,
    )


def split_body(groups):
    depth = groups // 4

    def flip_dp(values, bits):
        return lax.ppermute(values, "dp", [(i, i ^ bits) for i in range(groups)])

    def flip_core(values):
        return flip_dp(values, 1)

    def flip_y(values):
        return flip_dp(values, 2)

    def flip_x(values):
        return lax.ppermute(values, "shard", [(0, 1), (1, 0)])

    def body(
        hidden_in,
        cotangent,
        segment_ids,
        live_mask,
        attend_gain,
        attend_shift,
        feed_gain,
        feed_shift,
        triple_weight,
        triple_bias,
        output_weight,
        output_bias,
        expand_weight,
        expand_bias,
        reduce_weight,
        reduce_bias,
    ):
        row, width = hidden_in.shape
        side = lax.axis_index("shard")
        place = lax.axis_index("dp")
        core, y_at, z_at = place & 1, (place >> 1) & 1, place >> 2
        part = side * 2 + core
        heads = HEADS // 4
        cols = heads * HEAD
        hidden_units = expand_weight.shape[1] // 2
        half = width // 2

        def pair(mine, other, at, axis=0):
            first = jnp.where(at == 0, mine, other)
            second = jnp.where(at == 0, other, mine)
            return jnp.concatenate([first, second], axis=axis)

        def gather_rows(values):
            across = flip_x(values)
            return jnp.concatenate([values, flip_core(values), across, flip_core(across)], axis=0)

        def scatter_rows(values):
            parts = values.reshape(4, row, width)
            send = jnp.concatenate([parts[1], parts[3]], axis=0).astype(jnp.bfloat16)
            got = flip_core(send).astype(jnp.float32)
            mine = parts[0] + got[:row]
            theirs = parts[2] + got[row:]
            return mine + flip_x(theirs.astype(jnp.bfloat16)).astype(jnp.float32)

        hidden = gather_rows(hidden_in)
        marks = gather_rows(segment_ids * 2 + live_mask)
        segments, live = (marks >> 1).reshape(4, row), (marks & 1).reshape(4, row)
        cot = gather_rows(cotangent)

        vectors = jnp.stack([attend_gain, attend_shift, feed_gain, feed_shift, output_bias, reduce_bias])
        vectors_other = flip_x(vectors)
        full = pair(vectors, vectors_other, side, axis=1).astype(jnp.float32)
        gain_one, shift_one, gain_two, shift_two, output_bias_full, reduce_bias_full = full
        triple_bias_full = pair(triple_bias, flip_x(triple_bias), side).reshape(3, 4, cols)
        bias_mine = lax.dynamic_index_in_dim(triple_bias_full, part, 1, False).astype(jnp.float32)

        by_part = triple_weight.reshape(half, 3, 4, cols)
        triple_mine = lax.dynamic_index_in_dim(by_part, part, 1 + 1, False).reshape(half, 3 * cols)
        triple_send = lax.dynamic_index_in_dim(by_part, part ^ 2, 1 + 1, False).reshape(half, 3 * cols)
        triple_full = pair(triple_mine, flip_x(triple_send), side)
        output_mine = lax.dynamic_slice_in_dim(output_weight, core * cols, cols, 0)
        expand_mine = lax.dynamic_slice_in_dim(expand_weight, core * hidden_units, hidden_units, 1)
        reduce_mine = lax.dynamic_slice_in_dim(reduce_weight, core * hidden_units, hidden_units, 0)
        expand_bias_mine = lax.dynamic_slice_in_dim(
            expand_bias, core * hidden_units, hidden_units, 0
        ).astype(jnp.float32)

        inputs32 = hidden.astype(jnp.float32)
        normed, scale = normalize(inputs32)
        act_one = (normed * gain_one + shift_one).astype(jnp.bfloat16)
        act_two = (normed * gain_two + shift_two).astype(jnp.bfloat16)
        upstream_bf = jnp.where(live.reshape(4 * row, 1) > 0, cot, jnp.zeros_like(cot))

        feed_pre = product(act_two, expand_mine) + expand_bias_mine
        feed_hidden = smooth_gate(feed_pre).astype(jnp.bfloat16)
        feed = product(feed_hidden, reduce_mine)
        reduce_term = transposed_times(feed_hidden, upstream_bf).astype(jnp.bfloat16)
        pre_grad = times_transposed(upstream_bf, reduce_mine) * smooth_slope(feed_pre)
        pre_grad_bf = pre_grad.astype(jnp.bfloat16)
        expand_term = transposed_times(act_two, pre_grad_bf).astype(jnp.bfloat16)
        feed_input_grad = times_transposed(pre_grad_bf, expand_mine)

        cosine, sine = jax.vmap(rotary_tables)(segments)
        allowed = jax.vmap(allowed_mask)(segments, live)
        shaped = (4, row, heads, HEAD)
        triple = product(act_one, triple_full).reshape(4 * row, 3, cols) + bias_mine
        query = rotate(triple[:, 0].reshape(shaped), cosine, sine).astype(jnp.bfloat16)
        keys = rotate(triple[:, 1].reshape(shaped), cosine, sine).astype(jnp.bfloat16)
        values = triple[:, 2].reshape(shaped).astype(jnp.bfloat16)
        context, logsum = jax.vmap(attend)(query, keys, values, allowed)
        context_flat = context.reshape(4 * row, cols)
        attention = product(context_flat, output_mine)
        output_term = transposed_times(context_flat, upstream_bf).astype(jnp.bfloat16)
        context_grad = times_transposed(upstream_bf, output_mine).astype(jnp.bfloat16).reshape(shaped)
        query_grad, key_grad, value_grad = jax.vmap(attend_back)(
            query, keys, values, allowed, logsum, context_grad
        )
        triple_grad = jnp.concatenate(
            [
                rotate_back(query_grad, cosine, sine).reshape(4 * row, cols),
                rotate_back(key_grad, cosine, sine).reshape(4 * row, cols),
                value_grad.reshape(4 * row, cols),
            ],
            axis=1,
        )
        triple_grad_bf = triple_grad.astype(jnp.bfloat16)
        triple_term = transposed_times(act_one, triple_grad_bf).astype(jnp.bfloat16)
        attend_input_grad = times_transposed(triple_grad_bf, triple_full)

        own32 = inputs32[:row]
        block_out = (
            own32 + scatter_rows(attention + feed) + output_bias_full + reduce_bias_full
        ).astype(jnp.bfloat16)
        slope_sum = scatter_rows(attend_input_grad * gain_one + feed_input_grad * gain_two)
        own_normed, own_scale = normed[:row], scale[:row]
        upstream = upstream_bf[:row].astype(jnp.float32)
        input_slope = upstream + norm_back(slope_sum, own_normed, own_scale, 1.0)

        def reduce_pieces(term):
            keep = lax.dynamic_index_in_dim(term, y_at, 0, False)
            send = lax.dynamic_index_in_dim(term, 1 - y_at, 0, False)
            total = keep.astype(jnp.float32) + flip_y(send).astype(jnp.float32)
            total_bf = total.astype(jnp.bfloat16)
            result = lax.dynamic_index_in_dim(total, z_at, 0, False)
            for step in range(1, depth):
                piece = lax.dynamic_index_in_dim(total_bf, z_at ^ step, 0, False)
                result = result + flip_dp(piece, 4 * step).astype(jnp.float32)
            return result.astype(jnp.bfloat16)

        def gather_pieces(piece):
            whole = jnp.zeros((depth,) + piece.shape, piece.dtype)
            whole = lax.dynamic_update_index_in_dim(whole, piece, z_at, 0)
            for step in range(1, depth):
                whole = lax.dynamic_update_index_in_dim(
                    whole, flip_dp(piece, 4 * step), z_at ^ step, 0
                )
            both = pair(whole[None], flip_y(whole)[None], y_at)
            return both

        def joined(pieces, axis):
            return pair(pieces, flip_core(pieces), core, axis=axis)

        reduce_piece = reduce_pieces(reduce_term.reshape(2, depth, -1, width))
        expand_piece = reduce_pieces(expand_term.reshape(2, depth, -1, hidden_units))
        output_piece = reduce_pieces(output_term.reshape(2, depth, -1, width))
        split_rows = triple_term.reshape(2, 2, depth, -1, 3 * cols).transpose(1, 2, 0, 3, 4)
        triple_piece = reduce_pieces(split_rows)
        triple_keep = lax.dynamic_index_in_dim(triple_piece, side, 0, False)
        triple_pass = flip_x(lax.dynamic_index_in_dim(triple_piece, 1 - side, 0, False))
        triple_piece = pair(triple_keep[:, None], triple_pass[:, None], side, axis=1)

        reduce_sum = joined(gather_pieces(reduce_piece).reshape(hidden_units, width), 0)
        expand_sum = joined(gather_pieces(expand_piece).reshape(width, hidden_units), 1)
        output_sum = joined(gather_pieces(output_piece).reshape(cols, width), 0)
        triple_all = gather_pieces(triple_piece).reshape(half, 2, 3, 1, cols)
        triple_sum = joined(triple_all, 3).transpose(0, 2, 1, 3, 4).reshape(half, 12 * cols)

        triple_bias_term = jnp.sum(triple_grad, axis=0).reshape(3, 1, cols)
        triple_bias_term = lax.dynamic_update_slice(
            jnp.zeros((3, 4, cols), jnp.float32), triple_bias_term, (0, part, 0)
        )
        expand_bias_term = lax.dynamic_update_slice(
            jnp.zeros((4, hidden_units), jnp.float32), jnp.sum(pre_grad, axis=0)[None], (part, 0)
        )
        small = jnp.concatenate(
            [
                jnp.sum(attend_input_grad * normed, axis=0),
                jnp.sum(attend_input_grad, axis=0),
                jnp.sum(feed_input_grad * normed, axis=0),
                jnp.sum(feed_input_grad, axis=0),
                jnp.sum(upstream, axis=0),
                triple_bias_term.reshape(-1),
                expand_bias_term.reshape(-1),
            ]
        )
        small = small.reshape(-1, 128)
        small = small + flip_core(small)
        small = small + flip_x(small)
        bits = 2
        while bits < groups:
            small = small + flip_dp(small, bits)
            bits *= 2
        small = small.reshape(-1)

        def owned(start, size):
            return lax.dynamic_slice_in_dim(small, start + side * (size // 2), size // 2, 0)

        wide = 5 * width
        bias_sum = owned(4 * width, width)
        return (
            block_out,
            input_slope,
            owned(0, width),
            owned(width, width),
            owned(2 * width, width),
            owned(3 * width, width),
            triple_sum.astype(jnp.float32),
            owned(wide, 12 * cols),
            output_sum.astype(jnp.float32),
            bias_sum,
            expand_sum.astype(jnp.float32),
            owned(wide + 12 * cols, 4 * hidden_units),
            reduce_sum.astype(jnp.float32),
            bias_sum,
        )

    return body


def solution(mesh):
    placed = (
        P(("dp", "shard"), None),
        P(("dp", "shard"), None),
        P(("dp", "shard")),
        P(("dp", "shard")),
        P("shard"),
        P("shard"),
        P("shard"),
        P("shard"),
        P("shard", None),
        P("shard"),
        P("shard", None),
        P("shard"),
        P(None, "shard"),
        P("shard"),
        P("shard", None),
        P("shard"),
    )
    split = mesh.shape['shard'] == 2 and HEADS % 4 == 0
    whole_rows = mesh.shape['dp'] >= 8 and mesh.shape['dp'] & (mesh.shape['dp'] - 1) == 0
    body = split_body(mesh.shape['dp']) if split and whole_rows else gathered_body
    return jax.shard_map(
        body,
        mesh=mesh,
        in_specs=placed,
        out_specs=(
            P(("dp", "shard"), None),
            P(("dp", "shard"), None),
            P("shard"),
            P("shard"),
            P("shard"),
            P("shard"),
            P("shard", None),
            P("shard"),
            P("shard", None),
            P("shard"),
            P(None, "shard"),
            P("shard"),
            P("shard", None),
            P("shard"),
        ),
        check_vma=False,
    )
```

```python
import math

import jax
import jax.numpy as jnp
from jax import lax
from jax.experimental import pallas as pl
from jax.experimental.pallas import tpu as pltpu
from jax.sharding import PartitionSpec as P

HEADS = 12
HEAD = 64
ROT = 16


EPSILON = 1e-05
ROOT_HALF = 0.7071067811865476
DENSITY = 0.3989422804014327
NEGATIVE = -1e30


def product(left, right):
    return jnp.dot(left, right, preferred_element_type=jnp.float32)


def times_transposed(left, right):
    return lax.dot_general(
        left, right, (((1,), (1,)), ((), ())), preferred_element_type=jnp.float32
    )


def transposed_times(left, right):
    return lax.dot_general(
        left, right, (((0,), (0,)), ((), ())), preferred_element_type=jnp.float32
    )


def normalize(values):
    mean = jnp.mean(values, axis=-1, keepdims=True)
    centered = values - mean
    spread = jnp.mean(centered * centered, axis=-1, keepdims=True)
    scale = lax.rsqrt(spread + EPSILON)
    return (centered * scale, scale)


def norm_back(grad_out, normed, scale, gain):
    scaled = grad_out * gain
    first = jnp.mean(scaled, axis=-1, keepdims=True)
    second = jnp.mean(scaled * normed, axis=-1, keepdims=True)
    return scale * (scaled - first - normed * second)


def smooth_gate(values):
    return 0.5 * values * (1.0 + lax.erf(values * ROOT_HALF))


def smooth_slope(values):
    return 0.5 * (1.0 + lax.erf(values * ROOT_HALF)) + values * DENSITY * jnp.exp(
        -0.5 * values * values
    )


def rotary_tables(segment_row):
    count = segment_row.shape[0]
    index = jnp.arange(count)
    same = segment_row[:, None] == segment_row[None, :]
    before = index[None, :] < index[:, None]
    position = jnp.sum((same & before).astype(jnp.float32), axis=1)
    freqs = jnp.power(10000.0, -jnp.arange(0, ROT, 2).astype(jnp.float32) / ROT)
    angle = position[:, None] * freqs[None, :]
    angle = jnp.concatenate([angle, angle], axis=1)
    return (jnp.cos(angle), jnp.sin(angle))


def allowed_mask(segment_row, live_row):
    count = segment_row.shape[0]
    index = jnp.arange(count)
    same = segment_row[:, None] == segment_row[None, :]
    causal = index[None, :] <= index[:, None]
    both = (live_row[:, None] > 0) & (live_row[None, :] > 0)
    diagonal = index[:, None] == index[None, :]
    return same & causal & (both | diagonal)


def rotate(heads, cosine, sine):
    half = ROT // 2
    part = heads[..., :ROT]
    turned = jnp.concatenate([-part[..., half:], part[..., :half]], axis=-1)
    mixed = part * jnp.expand_dims(cosine, -2) + turned * jnp.expand_dims(sine, -2)
    return jnp.concatenate([mixed, heads[..., ROT:]], axis=-1)


def rotate_back(grads, cosine, sine):
    half = ROT // 2
    part = grads[..., :ROT]
    sined = part * jnp.expand_dims(sine, -2)
    turned = jnp.concatenate([sined[..., half:], -sined[..., :half]], axis=-1)
    mixed = part * jnp.expand_dims(cosine, -2) + turned
    return jnp.concatenate([mixed, grads[..., ROT:]], axis=-1)


def masked_scores(query, keys, allowed):
    scale = 1.0 / math.sqrt(HEAD)
    scores = jnp.einsum("qhd,khd->hqk", query, keys, preferred_element_type=jnp.float32) * scale
    return jnp.where(allowed[None], scores, NEGATIVE)


def attend(query, keys, values, allowed):
    scores = masked_scores(query, keys, allowed)
    top = jnp.max(scores, axis=-1, keepdims=True)
    total = jnp.sum(jnp.exp(scores - top), axis=-1, keepdims=True)
    logsum = top + jnp.log(total)
    probs = jnp.exp(scores - logsum).astype(jnp.bfloat16)
    context = jnp.einsum("hqk,khd->qhd", probs, values, preferred_element_type=jnp.float32)
    return (context.astype(jnp.bfloat16), logsum)


def attend_back(query, keys, values, allowed, logsum, context_grad):
    scale = 1.0 / math.sqrt(HEAD)
    probs = jnp.exp(masked_scores(query, keys, allowed) - logsum)
    probs_bf = probs.astype(jnp.bfloat16)
    value_grad = jnp.einsum(
        "hqk,qhd->khd", probs_bf, context_grad, preferred_element_type=jnp.float32
    )
    prob_grad = jnp.einsum("qhd,khd->hqk", context_grad, values, preferred_element_type=jnp.float32)
    delta = jnp.sum(probs * prob_grad, axis=-1, keepdims=True)
    score_grad = (probs * (prob_grad - delta) * scale).astype(jnp.bfloat16)
    query_grad = jnp.einsum("hqk,khd->qhd", score_grad, keys, preferred_element_type=jnp.float32)
    key_grad = jnp.einsum("hqk,qhd->khd", score_grad, query, preferred_element_type=jnp.float32)
    return (query_grad, key_grad, value_grad)


def gathered_body(
    hidden_in,
    cotangent,
    segment_ids,
    live_mask,
    attend_gain,
    attend_shift,
    feed_gain,
    feed_shift,
    triple_weight,
    triple_bias,
    output_weight,
    output_bias,
    expand_weight,
    expand_bias,
    reduce_weight,
    reduce_bias,
):
    tokens = hidden_in.shape[0]
    width = HEADS * HEAD
    shaped = (tokens, HEADS, HEAD)
    (
        gain_one,
        shift_one,
        gain_two,
        shift_two,
        triple_full,
        triple_bias_full,
        output_full,
        output_bias_full,
        reduce_bias_full,
    ) = (
        lax.all_gather(attend_gain, "shard", axis=0, tiled=True),
        lax.all_gather(attend_shift, "shard", axis=0, tiled=True),
        lax.all_gather(feed_gain, "shard", axis=0, tiled=True),
        lax.all_gather(feed_shift, "shard", axis=0, tiled=True),
        lax.all_gather(triple_weight, "shard", axis=0, tiled=True),
        lax.all_gather(triple_bias, "shard", axis=0, tiled=True),
        lax.all_gather(output_weight, "shard", axis=0, tiled=True),
        lax.all_gather(output_bias, "shard", axis=0, tiled=True),
        lax.all_gather(reduce_bias, "shard", axis=0, tiled=True),
    )
    inputs32 = hidden_in.astype(jnp.float32)
    normed, scale = normalize(inputs32)
    act_one = (normed * gain_one.astype(jnp.float32) + shift_one.astype(jnp.float32)).astype(
        jnp.bfloat16
    )
    act_two = (normed * gain_two.astype(jnp.float32) + shift_two.astype(jnp.float32)).astype(
        jnp.bfloat16
    )
    cosine, sine = rotary_tables(segment_ids)
    allowed = allowed_mask(segment_ids, live_mask)
    triple = product(act_one, triple_full) + triple_bias_full.astype(jnp.float32)
    query = rotate(triple[:, :width].reshape(shaped), cosine, sine).astype(jnp.bfloat16)
    keys = rotate(triple[:, width : 2 * width].reshape(shaped), cosine, sine).astype(jnp.bfloat16)
    values = triple[:, 2 * width :].reshape(shaped).astype(jnp.bfloat16)
    context, logsum = attend(query, keys, values, allowed)
    context_flat = context.reshape(tokens, width)
    attention = product(context_flat, output_full) + output_bias_full.astype(jnp.float32)
    expand_full, expand_bias_full, reduce_full = (
        lax.all_gather(expand_weight, "shard", axis=1, tiled=True),
        lax.all_gather(expand_bias, "shard", axis=0, tiled=True),
        lax.all_gather(reduce_weight, "shard", axis=0, tiled=True),
    )
    feed_pre = product(act_two, expand_full) + expand_bias_full.astype(jnp.float32)
    feed_hidden = smooth_gate(feed_pre).astype(jnp.bfloat16)
    feed = product(feed_hidden, reduce_full)
    block_out = (inputs32 + attention + feed + reduce_bias_full.astype(jnp.float32)).astype(
        jnp.bfloat16
    )
    upstream = cotangent.astype(jnp.float32) * live_mask.astype(jnp.float32)[:, None]
    upstream_bf = upstream.astype(jnp.bfloat16)
    gain_one_again, gain_two_again, triple_again, output_again = (
        lax.all_gather(attend_gain, "shard", axis=0, tiled=True),
        lax.all_gather(feed_gain, "shard", axis=0, tiled=True),
        lax.all_gather(triple_weight, "shard", axis=0, tiled=True),
        lax.all_gather(output_weight, "shard", axis=0, tiled=True),
    )
    expand_again, reduce_again = (
        lax.all_gather(expand_weight, "shard", axis=1, tiled=True),
        lax.all_gather(reduce_weight, "shard", axis=0, tiled=True),
    )
    pre_grad = times_transposed(upstream_bf, reduce_again) * smooth_slope(feed_pre)
    pre_grad_bf = pre_grad.astype(jnp.bfloat16)
    feed_input_grad = times_transposed(pre_grad_bf, expand_again)
    expand_term, expand_bias_term, reduce_term = (
        lax.psum_scatter(
            transposed_times(act_two, pre_grad_bf).astype(jnp.bfloat16),
            "shard",
            scatter_dimension=1,
            tiled=True,
        ).astype(jnp.float32),
        lax.psum_scatter(
            jnp.sum(pre_grad, axis=0).astype(jnp.bfloat16), "shard", scatter_dimension=0, tiled=True
        ).astype(jnp.float32),
        lax.psum_scatter(
            transposed_times(feed_hidden, upstream_bf).astype(jnp.bfloat16),
            "shard",
            scatter_dimension=0,
            tiled=True,
        ).astype(jnp.float32),
    )
    bias_term = jnp.sum(upstream, axis=0)
    output_term = transposed_times(context_flat, upstream_bf)
    context_grad = times_transposed(upstream_bf, output_again).astype(jnp.bfloat16).reshape(shaped)
    query_grad, key_grad, value_grad = attend_back(
        query, keys, values, allowed, logsum, context_grad
    )
    triple_grad = jnp.concatenate(
        [
            rotate_back(query_grad, cosine, sine).reshape(tokens, width),
            rotate_back(key_grad, cosine, sine).reshape(tokens, width),
            value_grad.reshape(tokens, width),
        ],
        axis=1,
    )
    triple_bias_term = jnp.sum(triple_grad, axis=0)
    triple_grad_bf = triple_grad.astype(jnp.bfloat16)
    triple_term = transposed_times(act_one, triple_grad_bf)
    attend_input_grad = times_transposed(triple_grad_bf, triple_again)
    gain_one_term = jnp.sum(attend_input_grad * normed, axis=0)
    shift_one_term = jnp.sum(attend_input_grad, axis=0)
    gain_two_term = jnp.sum(feed_input_grad * normed, axis=0)
    shift_two_term = jnp.sum(feed_input_grad, axis=0)
    input_slope = (
        upstream
        + norm_back(attend_input_grad, normed, scale, gain_one_again.astype(jnp.float32))
        + norm_back(feed_input_grad, normed, scale, gain_two_again.astype(jnp.float32))
    )
    (
        gain_one_part,
        shift_one_part,
        gain_two_part,
        shift_two_part,
        triple_part,
        triple_bias_part,
        output_part,
        bias_part,
    ) = (
        lax.psum_scatter(
            gain_one_term.astype(jnp.bfloat16), "shard", scatter_dimension=0, tiled=True
        ).astype(jnp.float32),
        lax.psum_scatter(
            shift_one_term.astype(jnp.bfloat16), "shard", scatter_dimension=0, tiled=True
        ).astype(jnp.float32),
        lax.psum_scatter(
            gain_two_term.astype(jnp.bfloat16), "shard", scatter_dimension=0, tiled=True
        ).astype(jnp.float32),
        lax.psum_scatter(
            shift_two_term.astype(jnp.bfloat16), "shard", scatter_dimension=0, tiled=True
        ).astype(jnp.float32),
        lax.psum_scatter(
            triple_term.astype(jnp.bfloat16), "shard", scatter_dimension=0, tiled=True
        ).astype(jnp.float32),
        lax.psum_scatter(
            triple_bias_term.astype(jnp.bfloat16), "shard", scatter_dimension=0, tiled=True
        ).astype(jnp.float32),
        lax.psum_scatter(
            output_term.astype(jnp.bfloat16), "shard", scatter_dimension=0, tiled=True
        ).astype(jnp.float32),
        lax.psum_scatter(
            bias_term.astype(jnp.bfloat16), "shard", scatter_dimension=0, tiled=True
        ).astype(jnp.float32),
    )
    (
        gain_one_sum,
        shift_one_sum,
        gain_two_sum,
        shift_two_sum,
        triple_sum,
        triple_bias_sum,
        output_sum,
        bias_sum,
        expand_sum,
        expand_bias_sum,
        reduce_sum,
    ) = (
        lax.psum(gain_one_part.astype(jnp.bfloat16), "dp").astype(jnp.float32),
        lax.psum(shift_one_part.astype(jnp.bfloat16), "dp").astype(jnp.float32),
        lax.psum(gain_two_part.astype(jnp.bfloat16), "dp").astype(jnp.float32),
        lax.psum(shift_two_part.astype(jnp.bfloat16), "dp").astype(jnp.float32),
        lax.psum(triple_part.astype(jnp.bfloat16), "dp").astype(jnp.float32),
        lax.psum(triple_bias_part.astype(jnp.bfloat16), "dp").astype(jnp.float32),
        lax.psum(output_part.astype(jnp.bfloat16), "dp").astype(jnp.float32),
        lax.psum(bias_part.astype(jnp.bfloat16), "dp").astype(jnp.float32),
        lax.psum(expand_term.astype(jnp.bfloat16), "dp").astype(jnp.float32),
        lax.psum(expand_bias_term.astype(jnp.bfloat16), "dp").astype(jnp.float32),
        lax.psum(reduce_term.astype(jnp.bfloat16), "dp").astype(jnp.float32),
    )
    return (
        block_out,
        input_slope,
        gain_one_sum,
        shift_one_sum,
        gain_two_sum,
        shift_two_sum,
        triple_sum,
        triple_bias_sum,
        output_sum,
        bias_sum,
        expand_sum,
        expand_bias_sum,
        reduce_sum,
        bias_sum,
    )


TILE = 256


def whole(memory_space=pltpu.VMEM):
    return pl.BlockSpec(memory_space=memory_space)


def local_call(kernel, outs, args, scratch=(), flops=0):
    moved = sum(math.prod(a.shape) * a.dtype.itemsize for a in (*args, *outs))
    return pl.pallas_call(
        kernel,
        out_shape=tuple(outs),
        in_specs=[whole(pltpu.SMEM)] + [whole()] * (len(args) - 1),
        out_specs=tuple(whole() for _ in outs),
        scratch_shapes=list(scratch),
        cost_estimate=pl.CostEstimate(flops=flops, bytes_accessed=moved, transcendentals=0),
        compiler_params=pltpu.CompilerParams(vmem_limit_bytes=60 * 1024 * 1024),
    )(*args)


def shape_of(*dims, dtype=jnp.bfloat16):
    return jax.ShapeDtypeStruct(dims, dtype)


def prepare_kernel(at, weight, mine, send):
    part = at[0] * 2 + at[1]
    cols = mine.shape[1] // 3
    heads = cols // HEAD

    def copy(target, where):
        for each in range(4):

            @pl.when(where == each)
            def _(each=each):
                for head in range(heads):
                    for kind in range(3):
                        start = kind * 4 * cols + each * cols + head * HEAD
                        to = head * 2 * HEAD + kind * HEAD if kind < 2 else 2 * cols + head * HEAD
                        target[:, to : to + HEAD] = weight[:, start : start + HEAD]

    copy(mine, part)
    copy(send, part ^ 2)


def feed_forward_kernel(
    at, h0, h1, h2, h3, u0, u1, u2, u3, vectors, expand, expand_bias, reduce,
    act_one, act_two, upstream, normed_out, scale_out, feed, slope, keep, send,
    hidden, feed_hidden, grads,
):
    row = h0.shape[0]
    units = slope.shape[1]
    mine = pl.ds(pl.multiple_of(at[1] * units, 128), units)
    for index, (h, u) in enumerate(((h0, u0), (h1, u1), (h2, u2), (h3, u3))):
        hidden[index * row : (index + 1) * row] = h[...]
        upstream[index * row : (index + 1) * row] = u[...]

    @pl.loop(0, 4 * row // TILE)
    def _(step):
        rows = pl.ds(pl.multiple_of(step * TILE, TILE), TILE)
        normed, scale = normalize(hidden[rows].astype(jnp.float32))
        normed_out[rows] = normed
        scale_out[rows] = jnp.broadcast_to(scale, (TILE, 128))
        act_one[rows] = (normed * vectors[0:1] + vectors[1:2]).astype(jnp.bfloat16)
        two = (normed * vectors[2:3] + vectors[3:4]).astype(jnp.bfloat16)
        act_two[rows] = two
        pre = product(two, expand[:, mine]) + expand_bias[...]
        bell = 0.5 * (1.0 + lax.erf(pre * ROOT_HALF))
        out = (pre * bell).astype(jnp.bfloat16)
        feed_hidden[rows] = out
        slope[rows] = bell + pre * DENSITY * jnp.exp(-0.5 * pre * pre)
        feed[rows] = product(out, reduce[mine])

    weight_grads(feed_hidden, upstream, grads)
    part_rows(at, grads, keep, send)


def weight_grads(left, right, grads):
    @pl.loop(0, right.shape[1] // TILE)
    def _(step):
        cols = pl.ds(pl.multiple_of(step * TILE, TILE), TILE)
        grads[:, cols] = transposed_times(left[...], right[:, cols])


def part_rows(at, grads, keep, send):
    parts, rows = keep.shape[0], keep.shape[1]
    for each in range(parts):
        start = each * 2 * rows
        keep[each] = grads[pl.ds(pl.multiple_of(start + at[2] * rows, 8), rows)]
        send[each] = grads[pl.ds(pl.multiple_of(start + (1 - at[2]) * rows, 8), rows)].astype(
            jnp.bfloat16
        )


def feed_backward_kernel(
    at, act_two, upstream, normed, slope, vectors, expand, reduce,
    slope_part, sums, keep, send,
    pre_grads, grads,
):
    units = slope.shape[1]
    mine = pl.ds(pl.multiple_of(at[1] * units, 128), units)
    sums[...] = jnp.zeros_like(sums)

    @pl.loop(0, act_two.shape[0] // TILE)
    def _(step):
        rows = pl.ds(pl.multiple_of(step * TILE, TILE), TILE)
        pre_grad = times_transposed(upstream[rows], reduce[mine]) * slope[rows]
        rounded = pre_grad.astype(jnp.bfloat16)
        pre_grads[rows] = rounded
        back = times_transposed(rounded, expand[:, mine])
        slope_part[rows] = back * vectors[2:3]
        sums[0:1] += jnp.sum(back * normed[rows], axis=0, keepdims=True)
        sums[1:2] += jnp.sum(back, axis=0, keepdims=True)
        sums[2:3] += jnp.sum(pre_grad, axis=0, keepdims=True)

    weight_grads(act_two, pre_grads, grads)
    part_rows(at, grads, keep, send)


def attention_kernel(
    at, keys_of, act_one, upstream, normed, feed, slope_part, vectors, cosine, sine_low, sine_high,
    mine, other, bias, output,
    out_keep, out_send, slope_keep, slope_send, sums, bias_sums, keep, send,
    weight, contexts, triple_grads, grads,
):
    row, width = act_one.shape[0] // 4, act_one.shape[1]
    half = mine.shape[0]
    cols = mine.shape[1] // 3
    heads = cols // HEAD
    weight[pl.ds(pl.multiple_of(at[0] * half, 128), half)] = mine[...]
    weight[pl.ds(pl.multiple_of((1 - at[0]) * half, 128), half)] = other[...]
    output_rows = pl.ds(pl.multiple_of(at[1] * cols, 64), cols)
    sums[...] = jnp.zeros_like(sums)
    bias_sums[...] = jnp.zeros_like(bias_sums)
    score_scale = 1.0 / math.sqrt(HEAD)

    @pl.loop(0, 4)
    def _(step):
        rows = pl.ds(pl.multiple_of(step * row, row), row)
        key_row = jnp.broadcast_to(keys_of[pl.ds(step, 1)], (row, row))
        key_column = key_row.T
        later = lax.broadcasted_iota(jnp.int32, (row, row), 0)
        earlier = lax.broadcasted_iota(jnp.int32, (row, row), 1)
        allowed = (key_row == key_column) & (earlier <= later)
        cos, low, high = cosine[rows], sine_low[rows], sine_high[rows]

        triple = product(act_one[rows], weight[...]) + bias[...]
        context_grads = times_transposed(upstream[rows], output[output_rows]).astype(jnp.bfloat16)
        for head in range(heads):
            pair = triple[:, head * 2 * HEAD : (head + 1) * 2 * HEAD]
            turned = pair * cos + pltpu.roll(pair, 2 * HEAD - ROT // 2, 1) * low
            turned = (turned + pltpu.roll(pair, ROT // 2, 1) * high).astype(jnp.bfloat16)
            query, keys = turned[:, :HEAD], turned[:, HEAD:]
            at_head = slice(head * HEAD, (head + 1) * HEAD)
            values = triple[:, 2 * cols + head * HEAD : 2 * cols + (head + 1) * HEAD].astype(
                jnp.bfloat16
            )
            scores = jnp.where(allowed, times_transposed(query, keys) * score_scale, NEGATIVE)
            top = jnp.max(scores, axis=-1, keepdims=True)
            weights = jnp.exp(scores - top)
            probs = weights / jnp.sum(weights, axis=-1, keepdims=True)
            probs_bf = probs.astype(jnp.bfloat16)
            contexts[rows, at_head] = product(probs_bf, values).astype(jnp.bfloat16)
            context_grad = context_grads[:, at_head]
            value_grad = transposed_times(probs_bf, context_grad)
            prob_grad = times_transposed(context_grad, values)
            delta = jnp.sum(probs * prob_grad, axis=-1, keepdims=True)
            score_grad = (probs * (prob_grad - delta) * score_scale).astype(jnp.bfloat16)
            query_grad = product(score_grad, keys)
            key_grad = transposed_times(score_grad, query)
            grad = jnp.concatenate([query_grad, key_grad], axis=1)
            back = grad * cos - pltpu.roll(grad, 2 * HEAD - ROT // 2, 1) * low
            back = back - pltpu.roll(grad, ROT // 2, 1) * high
            at_pair = slice(head * 2 * HEAD, (head + 1) * 2 * HEAD)
            at_value = slice(2 * cols + head * HEAD, 2 * cols + (head + 1) * HEAD)
            triple_grads[rows, at_pair] = back.astype(jnp.bfloat16)
            triple_grads[rows, at_value] = value_grad.astype(jnp.bfloat16)
            bias_sums[0:1, at_pair] += jnp.sum(back, axis=0, keepdims=True)
            bias_sums[0:1, at_value] += jnp.sum(value_grad, axis=0, keepdims=True)

        out = product(contexts[rows], output[output_rows]) + feed[rows]
        back = times_transposed(triple_grads[rows], weight[...])
        sums[0:1] += jnp.sum(back * normed[rows], axis=0, keepdims=True)
        sums[1:2] += jnp.sum(back, axis=0, keepdims=True)
        slope = back * vectors[0:1] + slope_part[rows]
        to = pl.ds(pl.multiple_of((step // 2) * row, row), row)

        @pl.when(step % 2 == 0)
        def _():
            out_keep[to] = out
            slope_keep[to] = slope

        @pl.when(step % 2 == 1)
        def _():
            out_send[to] = out.astype(jnp.bfloat16)
            slope_send[to] = slope.astype(jnp.bfloat16)

    @pl.loop(0, width // TILE)
    def _(step):
        some = pl.ds(pl.multiple_of(step * TILE, TILE), TILE)
        grads[some, : 3 * cols] = transposed_times(act_one[:, some], triple_grads[...])
        grads[some, 3 * cols :] = transposed_times(upstream[:, some], contexts[...])

    part_rows(at, grads, keep, send)


def split_kernel(at, keep, got, own, *sends):
    parts, rows = own.shape[0], own.shape[1]
    for each in range(parts):
        for step in range(len(sends) + 1):
            some = pl.ds(pl.multiple_of((at[3] ^ step) * rows, 16), rows)
            total = keep[each, some] + got[each, some].astype(jnp.float32)
            if step == 0:
                own[each] = total
            else:
                sends[step - 1][each] = total.astype(jnp.bfloat16)


def assemble_kernel(at, *refs):
    *pieces, out = refs
    count, rows = len(pieces) // 2, pieces[0].shape[0]
    for side in range(2):
        for step in range(count):
            start = ((at[2] ^ side) * count + (at[3] ^ step)) * rows
            out[pl.ds(pl.multiple_of(start, 16), rows)] = pieces[side * count + step][...]


def finish_rows_kernel(at, mine, other, out):
    rows = mine.shape[0]
    out[pl.ds(pl.multiple_of(at[1] * rows, 16), rows)] = mine[...].astype(jnp.float32)
    out[pl.ds(pl.multiple_of((1 - at[1]) * rows, 16), rows)] = other[...].astype(jnp.float32)


def finish_columns_kernel(at, mine, other, out):
    cols = mine.shape[1]
    out[:, pl.ds(pl.multiple_of(at[1] * cols, 128), cols)] = mine[...].astype(jnp.float32)
    out[:, pl.ds(pl.multiple_of((1 - at[1]) * cols, 128), cols)] = other[...].astype(jnp.float32)


def finish_attention_kernel(at, mine, other, triple, output):
    half = triple.shape[0]
    cols = triple.shape[1] // 12
    heads = cols // HEAD

    def place(source, core):
        for side in range(2):
            part = side * 2 + core
            base = side * 3 * cols
            for head in range(heads):
                for kind in range(3):
                    start = head * 2 * HEAD + kind * HEAD if kind < 2 else 2 * cols + head * HEAD
                    to = kind * 4 * cols + part * cols + head * HEAD
                    triple[:, to : to + HEAD] = source[:, base + start : base + start + HEAD].astype(
                        jnp.float32
                    )
            turned = source[:, 6 * cols + side * cols : 6 * cols + (side + 1) * cols]
            output[core * cols : (core + 1) * cols, side * half : (side + 1) * half] = turned.astype(
                jnp.float32
            ).T

    for core in range(2):

        @pl.when(at[1] == core)
        def _(core=core):
            place(mine, core)
            place(other, 1 - core)


def rotary_lanes(segments):
    count = segments.shape[1]
    index = jnp.arange(count)
    same = segments[:, :, None] == segments[:, None, :]
    before = index[:, None] < index[None, :]
    position = jnp.sum((same & before).astype(jnp.float32), axis=1).reshape(-1)
    freqs = jnp.power(10000.0, -jnp.arange(0, ROT, 2).astype(jnp.float32) / ROT)
    angle = freqs[:, None] * position[None, :]
    cos, sin = jnp.cos(angle), jnp.sin(angle)
    none, one = jnp.zeros_like(cos), jnp.ones((HEAD - ROT, angle.shape[1]), jnp.float32)

    def lanes(low, high, rest):
        return jnp.concatenate([low, high, rest, low, high, rest], axis=0).T

    return lanes(cos, cos, one), lanes(-sin, none, 0.0 * one), lanes(none, sin, 0.0 * one)


def split_body(groups):
    depth = groups // 4

    def flip_dp(values, bits):
        return lax.ppermute(values, "dp", [(i, i ^ bits) for i in range(groups)])

    def flip_core(values):
        return flip_dp(values, 1)

    def flip_y(values):
        return flip_dp(values, 2)

    def flip_x(values):
        return lax.ppermute(values, "shard", [(0, 1), (1, 0)])

    def body(
        hidden_in,
        cotangent,
        segment_ids,
        live_mask,
        attend_gain,
        attend_shift,
        feed_gain,
        feed_shift,
        triple_weight,
        triple_bias,
        output_weight,
        output_bias,
        expand_weight,
        expand_bias,
        reduce_weight,
        reduce_bias,
    ):
        row, width = hidden_in.shape
        tokens = 4 * row
        side = lax.axis_index("shard")
        place = lax.axis_index("dp")
        core = place & 1
        part = side * 2 + core
        at = jnp.stack([side, core, (place >> 1) & 1, place >> 2]).astype(jnp.int32)
        cols = triple_weight.shape[1] // 12
        units = expand_weight.shape[1] // 2
        half = width // 2
        f32 = jnp.float32

        def pair(mine, other, which, axis=0):
            first = jnp.where(which == 0, mine, other)
            second = jnp.where(which == 0, other, mine)
            return jnp.concatenate([first, second], axis=axis)

        def gather_rows(values):
            across = flip_x(values)
            return values, flip_core(values), across, flip_core(across)

        upstream_own = jnp.where(live_mask[:, None] > 0, cotangent, jnp.zeros_like(cotangent))
        hidden = gather_rows(hidden_in)
        upstreams = gather_rows(upstream_own)
        keys_own = jnp.where(live_mask > 0, segment_ids, 8 + jnp.arange(row))
        marks = jnp.stack([segment_ids, keys_own]).astype(f32)
        marks = jnp.stack(gather_rows(marks))

        vectors = [attend_gain, attend_shift, feed_gain, feed_shift, output_bias, reduce_bias]
        vectors = jnp.concatenate(vectors + [triple_bias])
        vectors_other = flip_x(vectors)
        six = [v[: 6 * half].reshape(6, half) for v in (vectors, vectors_other)]
        full = pair(*six, side, axis=1).astype(f32)
        bias = pair(vectors[6 * half :], vectors_other[6 * half :], side).reshape(3, 4, cols)
        bias = lax.dynamic_index_in_dim(bias, part, 1, False).reshape(3, cols // HEAD, HEAD)
        bias_pairs = bias[:2].transpose(1, 0, 2).reshape(1, 2 * cols)
        bias = jnp.concatenate([bias_pairs, bias[2].reshape(1, cols)], axis=1).astype(f32)
        expand_bias_mine = lax.dynamic_slice_in_dim(expand_bias, core * units, units, 0)
        expand_bias_mine = expand_bias_mine.astype(f32)[None]

        triple_mine, triple_send = local_call(
            prepare_kernel, [shape_of(half, 3 * cols)] * 2, (at, triple_weight)
        )
        triple_other = flip_x(triple_send)
        cosine, sine_low, sine_high = rotary_lanes(marks[:, 0])

        keep_shape = shape_of(1, half, width, dtype=f32)
        send_shape = shape_of(1, half, width)
        flops = 2 * tokens * width * units
        act_one, act_two, upstream, normed, scale, feed, slope, *reduce_parts = local_call(
            feed_forward_kernel,
            [
                shape_of(tokens, width),
                shape_of(tokens, width),
                shape_of(tokens, width),
                shape_of(tokens, width, dtype=f32),
                shape_of(tokens, 128, dtype=f32),
                shape_of(tokens, width, dtype=f32),
                shape_of(tokens, units, dtype=f32),
                keep_shape,
                send_shape,
            ],
            (at, *hidden, *upstreams, full, expand_weight, expand_bias_mine, reduce_weight),
            [
                pltpu.VMEM((tokens, width), jnp.bfloat16),
                pltpu.VMEM((tokens, units), jnp.bfloat16),
                pltpu.VMEM((units, width), f32),
            ],
            3 * flops,
        )
        slope_part, feed_sums, *expand_parts = local_call(
            feed_backward_kernel,
            [
                shape_of(tokens, width, dtype=f32),
                shape_of(8, width, dtype=f32),
                keep_shape,
                send_shape,
            ],
            (at, act_two, upstream, normed, slope, full, expand_weight, reduce_weight),
            [pltpu.VMEM((tokens, units), jnp.bfloat16), pltpu.VMEM((width, units), f32)],
            3 * flops,
        )
        (
            out_keep, out_send, slope_keep, slope_send, attend_sums, bias_sums, *triple_parts
        ) = local_call(
            attention_kernel,
            [
                shape_of(2 * row, width, dtype=f32),
                shape_of(2 * row, width),
                shape_of(2 * row, width, dtype=f32),
                shape_of(2 * row, width),
                shape_of(8, width, dtype=f32),
                shape_of(8, 3 * cols, dtype=f32),
                shape_of(2, half // 2, width, dtype=f32),
                shape_of(2, half // 2, width),
            ],
            (
                at, marks[:, 1], act_one, upstream, normed, feed, slope_part, full,
                cosine, sine_low, sine_high, triple_mine, triple_other, bias, output_weight,
            ),
            [
                pltpu.VMEM((width, 3 * cols), jnp.bfloat16),
                pltpu.VMEM((tokens, cols), jnp.bfloat16),
                pltpu.VMEM((tokens, 3 * cols), jnp.bfloat16),
                pltpu.VMEM((width, 4 * cols), f32),
            ],
            4 * flops,
        )

        def scatter_rows(keep, send):
            total = keep + flip_core(send).astype(f32)
            return total[:row] + flip_x(total[row:].astype(jnp.bfloat16)).astype(f32)

        block_out = (
            hidden_in.astype(f32) + scatter_rows(out_keep, out_send) + full[4] + full[5]
        ).astype(jnp.bfloat16)
        input_slope = upstream_own.astype(f32) + norm_back(
            scatter_rows(slope_keep, slope_send), normed[:row], scale[:row, :1], 1.0
        )

        def reduce_pieces(keep, send):
            parts, rows, _ = keep.shape
            piece = (parts, rows // depth, width)
            own, *sends = local_call(
                split_kernel,
                [shape_of(*piece, dtype=f32)] + [shape_of(*piece)] * (depth - 1),
                (at, keep, flip_y(send)),
            )
            for step in range(1, depth):
                own = own + flip_dp(sends[step - 1], 4 * step).astype(f32)
            return own.astype(jnp.bfloat16)

        def gather_pieces(piece):
            pieces = [piece] + [flip_dp(piece, 4 * step) for step in range(1, depth)]
            pieces = pieces + [flip_y(each) for each in pieces]
            shape = shape_of(piece.shape[0] * 2 * depth, piece.shape[1])
            (mine,) = local_call(assemble_kernel, [shape], (at, *pieces))
            return at, mine, flip_core(mine)

        reduce_piece = reduce_pieces(*reduce_parts)[0]
        expand_piece = reduce_pieces(*expand_parts)[0]
        triple_piece = reduce_pieces(*triple_parts)
        passed = lax.dynamic_index_in_dim(triple_piece[:, :, : 3 * cols], 1 - side, 0, False)
        kept = lax.dynamic_index_in_dim(triple_piece[:, :, : 3 * cols], side, 0, False)
        triple_piece = jnp.concatenate(
            [
                pair(kept, flip_x(passed), side, axis=1),
                triple_piece[0, :, 3 * cols :],
                triple_piece[1, :, 3 * cols :],
            ],
            axis=1,
        )
        (reduce_sum,) = local_call(
            finish_rows_kernel, [shape_of(2 * units, width, dtype=f32)], gather_pieces(reduce_piece)
        )
        (expand_sum,) = local_call(
            finish_columns_kernel,
            [shape_of(width, 2 * units, dtype=f32)],
            gather_pieces(expand_piece),
        )
        triple_sum, output_sum = local_call(
            finish_attention_kernel,
            [shape_of(half, 12 * cols, dtype=f32), shape_of(2 * cols, width, dtype=f32)],
            gather_pieces(triple_piece),
        )

        mine = (jnp.arange(4) == part).astype(f32)[:, None]
        small = jnp.concatenate(
            [
                attend_sums[:2],
                feed_sums[:2],
                jnp.sum(upstream_own.astype(f32), axis=0)[None],
                mine * feed_sums[2:3],
                mine * jnp.pad(bias_sums[:1], ((0, 0), (0, width - 3 * cols))),
                jnp.zeros((3, width), f32),
            ]
        )
        small = small + flip_core(small)
        small = small + flip_x(small)
        bits = 2
        while bits < groups:
            small = small + flip_dp(small, bits)
            bits *= 2
        owned = lax.dynamic_slice_in_dim(small[:5], side * half, half, 1)
        expand_bias_sum = lax.dynamic_slice_in_dim(small[5:9].reshape(-1), side * 2 * units, 2 * units, 0)
        bias_all = small[9:13, : 3 * cols]
        pairs = bias_all[:, : 2 * cols].reshape(4, cols // HEAD, 2, HEAD).transpose(2, 0, 1, 3)
        bias_all = jnp.concatenate([pairs.reshape(-1), bias_all[:, 2 * cols :].reshape(-1)])
        bias_sum = lax.dynamic_slice_in_dim(bias_all, side * 6 * cols, 6 * cols, 0)
        return (
            block_out,
            input_slope,
            owned[0],
            owned[1],
            owned[2],
            owned[3],
            triple_sum,
            bias_sum,
            output_sum,
            owned[4],
            expand_sum,
            expand_bias_sum,
            reduce_sum,
            owned[4],
        )

    return body


def solution(mesh):
    placed = (
        P(("dp", "shard"), None),
        P(("dp", "shard"), None),
        P(("dp", "shard")),
        P(("dp", "shard")),
        P("shard"),
        P("shard"),
        P("shard"),
        P("shard"),
        P("shard", None),
        P("shard"),
        P("shard", None),
        P("shard"),
        P(None, "shard"),
        P("shard"),
        P("shard", None),
        P("shard"),
    )
    split = mesh.shape['shard'] == 2 and HEADS % 4 == 0
    whole_rows = mesh.shape['dp'] >= 8 and mesh.shape['dp'] & (mesh.shape['dp'] - 1) == 0
    body = split_body(mesh.shape['dp']) if split and whole_rows else gathered_body
    return jax.shard_map(
        body,
        mesh=mesh,
        in_specs=placed,
        out_specs=(
            P(("dp", "shard"), None),
            P(("dp", "shard"), None),
            P("shard"),
            P("shard"),
            P("shard"),
            P("shard"),
            P("shard", None),
            P("shard"),
            P("shard", None),
            P("shard"),
            P(None, "shard"),
            P("shard"),
            P("shard", None),
            P("shard"),
        ),
        check_vma=False,
    )
```

```python
import functools
import math

import jax
import jax.numpy as jnp
import numpy as np
from jax import lax
from jax.experimental import pallas as pl
from jax.experimental.pallas import tpu as pltpu
from jax.sharding import PartitionSpec as P


HEADS = 12
HEAD = 64
ROT = 16


EPSILON = 1e-05
ROOT_HALF = 0.7071067811865476
DENSITY = 0.3989422804014327
NEGATIVE = -1e30


def product(left, right):
    return jnp.dot(left, right, preferred_element_type=jnp.float32)


def times_transposed(left, right):
    return lax.dot_general(
        left, right, (((1,), (1,)), ((), ())), preferred_element_type=jnp.float32
    )


def transposed_times(left, right):
    return lax.dot_general(
        left, right, (((0,), (0,)), ((), ())), preferred_element_type=jnp.float32
    )


def normalize(values):
    mean = jnp.mean(values, axis=-1, keepdims=True)
    centered = values - mean
    spread = jnp.mean(centered * centered, axis=-1, keepdims=True)
    scale = lax.rsqrt(spread + EPSILON)
    return (centered * scale, scale)


def norm_back(grad_out, normed, scale, gain):
    scaled = grad_out * gain
    first = jnp.mean(scaled, axis=-1, keepdims=True)
    second = jnp.mean(scaled * normed, axis=-1, keepdims=True)
    return scale * (scaled - first - normed * second)


def smooth_gate(values):
    return 0.5 * values * (1.0 + lax.erf(values * ROOT_HALF))


def smooth_slope(values):
    return 0.5 * (1.0 + lax.erf(values * ROOT_HALF)) + values * DENSITY * jnp.exp(
        -0.5 * values * values
    )


def rotary_tables(segment_row):
    count = segment_row.shape[0]
    index = jnp.arange(count)
    same = segment_row[:, None] == segment_row[None, :]
    before = index[None, :] < index[:, None]
    position = jnp.sum((same & before).astype(jnp.float32), axis=1)
    freqs = jnp.power(10000.0, -jnp.arange(0, ROT, 2).astype(jnp.float32) / ROT)
    angle = position[:, None] * freqs[None, :]
    angle = jnp.concatenate([angle, angle], axis=1)
    return (jnp.cos(angle), jnp.sin(angle))


def allowed_mask(segment_row, live_row):
    count = segment_row.shape[0]
    index = jnp.arange(count)
    same = segment_row[:, None] == segment_row[None, :]
    causal = index[None, :] <= index[:, None]
    both = (live_row[:, None] > 0) & (live_row[None, :] > 0)
    diagonal = index[:, None] == index[None, :]
    return same & causal & (both | diagonal)


def rotate(heads, cosine, sine):
    half = ROT // 2
    part = heads[..., :ROT]
    turned = jnp.concatenate([-part[..., half:], part[..., :half]], axis=-1)
    mixed = part * jnp.expand_dims(cosine, -2) + turned * jnp.expand_dims(sine, -2)
    return jnp.concatenate([mixed, heads[..., ROT:]], axis=-1)


def rotate_back(grads, cosine, sine):
    half = ROT // 2
    part = grads[..., :ROT]
    sined = part * jnp.expand_dims(sine, -2)
    turned = jnp.concatenate([sined[..., half:], -sined[..., :half]], axis=-1)
    mixed = part * jnp.expand_dims(cosine, -2) + turned
    return jnp.concatenate([mixed, grads[..., ROT:]], axis=-1)


def masked_scores(query, keys, allowed):
    scale = 1.0 / math.sqrt(HEAD)
    scores = jnp.einsum("qhd,khd->hqk", query, keys, preferred_element_type=jnp.float32) * scale
    return jnp.where(allowed[None], scores, NEGATIVE)


def attend(query, keys, values, allowed):
    scores = masked_scores(query, keys, allowed)
    top = jnp.max(scores, axis=-1, keepdims=True)
    total = jnp.sum(jnp.exp(scores - top), axis=-1, keepdims=True)
    logsum = top + jnp.log(total)
    probs = jnp.exp(scores - logsum).astype(jnp.bfloat16)
    context = jnp.einsum("hqk,khd->qhd", probs, values, preferred_element_type=jnp.float32)
    return (context.astype(jnp.bfloat16), logsum)


def attend_back(query, keys, values, allowed, logsum, context_grad):
    scale = 1.0 / math.sqrt(HEAD)
    probs = jnp.exp(masked_scores(query, keys, allowed) - logsum)
    probs_bf = probs.astype(jnp.bfloat16)
    value_grad = jnp.einsum(
        "hqk,qhd->khd", probs_bf, context_grad, preferred_element_type=jnp.float32
    )
    prob_grad = jnp.einsum("qhd,khd->hqk", context_grad, values, preferred_element_type=jnp.float32)
    delta = jnp.sum(probs * prob_grad, axis=-1, keepdims=True)
    score_grad = (probs * (prob_grad - delta) * scale).astype(jnp.bfloat16)
    query_grad = jnp.einsum("hqk,khd->qhd", score_grad, keys, preferred_element_type=jnp.float32)
    key_grad = jnp.einsum("hqk,qhd->khd", score_grad, query, preferred_element_type=jnp.float32)
    return (query_grad, key_grad, value_grad)


def gathered_body(
    hidden_in,
    cotangent,
    segment_ids,
    live_mask,
    attend_gain,
    attend_shift,
    feed_gain,
    feed_shift,
    triple_weight,
    triple_bias,
    output_weight,
    output_bias,
    expand_weight,
    expand_bias,
    reduce_weight,
    reduce_bias,
):
    tokens = hidden_in.shape[0]
    width = HEADS * HEAD
    shaped = (tokens, HEADS, HEAD)
    (
        gain_one,
        shift_one,
        gain_two,
        shift_two,
        triple_full,
        triple_bias_full,
        output_full,
        output_bias_full,
        reduce_bias_full,
    ) = (
        lax.all_gather(attend_gain, "shard", axis=0, tiled=True),
        lax.all_gather(attend_shift, "shard", axis=0, tiled=True),
        lax.all_gather(feed_gain, "shard", axis=0, tiled=True),
        lax.all_gather(feed_shift, "shard", axis=0, tiled=True),
        lax.all_gather(triple_weight, "shard", axis=0, tiled=True),
        lax.all_gather(triple_bias, "shard", axis=0, tiled=True),
        lax.all_gather(output_weight, "shard", axis=0, tiled=True),
        lax.all_gather(output_bias, "shard", axis=0, tiled=True),
        lax.all_gather(reduce_bias, "shard", axis=0, tiled=True),
    )
    inputs32 = hidden_in.astype(jnp.float32)
    normed, scale = normalize(inputs32)
    act_one = (normed * gain_one.astype(jnp.float32) + shift_one.astype(jnp.float32)).astype(
        jnp.bfloat16
    )
    act_two = (normed * gain_two.astype(jnp.float32) + shift_two.astype(jnp.float32)).astype(
        jnp.bfloat16
    )
    cosine, sine = rotary_tables(segment_ids)
    allowed = allowed_mask(segment_ids, live_mask)
    triple = product(act_one, triple_full) + triple_bias_full.astype(jnp.float32)
    query = rotate(triple[:, :width].reshape(shaped), cosine, sine).astype(jnp.bfloat16)
    keys = rotate(triple[:, width : 2 * width].reshape(shaped), cosine, sine).astype(jnp.bfloat16)
    values = triple[:, 2 * width :].reshape(shaped).astype(jnp.bfloat16)
    context, logsum = attend(query, keys, values, allowed)
    context_flat = context.reshape(tokens, width)
    attention = product(context_flat, output_full) + output_bias_full.astype(jnp.float32)
    expand_full, expand_bias_full, reduce_full = (
        lax.all_gather(expand_weight, "shard", axis=1, tiled=True),
        lax.all_gather(expand_bias, "shard", axis=0, tiled=True),
        lax.all_gather(reduce_weight, "shard", axis=0, tiled=True),
    )
    feed_pre = product(act_two, expand_full) + expand_bias_full.astype(jnp.float32)
    feed_hidden = smooth_gate(feed_pre).astype(jnp.bfloat16)
    feed = product(feed_hidden, reduce_full)
    block_out = (inputs32 + attention + feed + reduce_bias_full.astype(jnp.float32)).astype(
        jnp.bfloat16
    )
    upstream = cotangent.astype(jnp.float32) * live_mask.astype(jnp.float32)[:, None]
    upstream_bf = upstream.astype(jnp.bfloat16)
    gain_one_again, gain_two_again, triple_again, output_again = (
        lax.all_gather(attend_gain, "shard", axis=0, tiled=True),
        lax.all_gather(feed_gain, "shard", axis=0, tiled=True),
        lax.all_gather(triple_weight, "shard", axis=0, tiled=True),
        lax.all_gather(output_weight, "shard", axis=0, tiled=True),
    )
    expand_again, reduce_again = (
        lax.all_gather(expand_weight, "shard", axis=1, tiled=True),
        lax.all_gather(reduce_weight, "shard", axis=0, tiled=True),
    )
    pre_grad = times_transposed(upstream_bf, reduce_again) * smooth_slope(feed_pre)
    pre_grad_bf = pre_grad.astype(jnp.bfloat16)
    feed_input_grad = times_transposed(pre_grad_bf, expand_again)
    expand_term, expand_bias_term, reduce_term = (
        lax.psum_scatter(
            transposed_times(act_two, pre_grad_bf).astype(jnp.bfloat16),
            "shard",
            scatter_dimension=1,
            tiled=True,
        ).astype(jnp.float32),
        lax.psum_scatter(
            jnp.sum(pre_grad, axis=0).astype(jnp.bfloat16), "shard", scatter_dimension=0, tiled=True
        ).astype(jnp.float32),
        lax.psum_scatter(
            transposed_times(feed_hidden, upstream_bf).astype(jnp.bfloat16),
            "shard",
            scatter_dimension=0,
            tiled=True,
        ).astype(jnp.float32),
    )
    bias_term = jnp.sum(upstream, axis=0)
    output_term = transposed_times(context_flat, upstream_bf)
    context_grad = times_transposed(upstream_bf, output_again).astype(jnp.bfloat16).reshape(shaped)
    query_grad, key_grad, value_grad = attend_back(
        query, keys, values, allowed, logsum, context_grad
    )
    triple_grad = jnp.concatenate(
        [
            rotate_back(query_grad, cosine, sine).reshape(tokens, width),
            rotate_back(key_grad, cosine, sine).reshape(tokens, width),
            value_grad.reshape(tokens, width),
        ],
        axis=1,
    )
    triple_bias_term = jnp.sum(triple_grad, axis=0)
    triple_grad_bf = triple_grad.astype(jnp.bfloat16)
    triple_term = transposed_times(act_one, triple_grad_bf)
    attend_input_grad = times_transposed(triple_grad_bf, triple_again)
    gain_one_term = jnp.sum(attend_input_grad * normed, axis=0)
    shift_one_term = jnp.sum(attend_input_grad, axis=0)
    gain_two_term = jnp.sum(feed_input_grad * normed, axis=0)
    shift_two_term = jnp.sum(feed_input_grad, axis=0)
    input_slope = (
        upstream
        + norm_back(attend_input_grad, normed, scale, gain_one_again.astype(jnp.float32))
        + norm_back(feed_input_grad, normed, scale, gain_two_again.astype(jnp.float32))
    )
    (
        gain_one_part,
        shift_one_part,
        gain_two_part,
        shift_two_part,
        triple_part,
        triple_bias_part,
        output_part,
        bias_part,
    ) = (
        lax.psum_scatter(
            gain_one_term.astype(jnp.bfloat16), "shard", scatter_dimension=0, tiled=True
        ).astype(jnp.float32),
        lax.psum_scatter(
            shift_one_term.astype(jnp.bfloat16), "shard", scatter_dimension=0, tiled=True
        ).astype(jnp.float32),
        lax.psum_scatter(
            gain_two_term.astype(jnp.bfloat16), "shard", scatter_dimension=0, tiled=True
        ).astype(jnp.float32),
        lax.psum_scatter(
            shift_two_term.astype(jnp.bfloat16), "shard", scatter_dimension=0, tiled=True
        ).astype(jnp.float32),
        lax.psum_scatter(
            triple_term.astype(jnp.bfloat16), "shard", scatter_dimension=0, tiled=True
        ).astype(jnp.float32),
        lax.psum_scatter(
            triple_bias_term.astype(jnp.bfloat16), "shard", scatter_dimension=0, tiled=True
        ).astype(jnp.float32),
        lax.psum_scatter(
            output_term.astype(jnp.bfloat16), "shard", scatter_dimension=0, tiled=True
        ).astype(jnp.float32),
        lax.psum_scatter(
            bias_term.astype(jnp.bfloat16), "shard", scatter_dimension=0, tiled=True
        ).astype(jnp.float32),
    )
    (
        gain_one_sum,
        shift_one_sum,
        gain_two_sum,
        shift_two_sum,
        triple_sum,
        triple_bias_sum,
        output_sum,
        bias_sum,
        expand_sum,
        expand_bias_sum,
        reduce_sum,
    ) = (
        lax.psum(gain_one_part.astype(jnp.bfloat16), "dp").astype(jnp.float32),
        lax.psum(shift_one_part.astype(jnp.bfloat16), "dp").astype(jnp.float32),
        lax.psum(gain_two_part.astype(jnp.bfloat16), "dp").astype(jnp.float32),
        lax.psum(shift_two_part.astype(jnp.bfloat16), "dp").astype(jnp.float32),
        lax.psum(triple_part.astype(jnp.bfloat16), "dp").astype(jnp.float32),
        lax.psum(triple_bias_part.astype(jnp.bfloat16), "dp").astype(jnp.float32),
        lax.psum(output_part.astype(jnp.bfloat16), "dp").astype(jnp.float32),
        lax.psum(bias_part.astype(jnp.bfloat16), "dp").astype(jnp.float32),
        lax.psum(expand_term.astype(jnp.bfloat16), "dp").astype(jnp.float32),
        lax.psum(expand_bias_term.astype(jnp.bfloat16), "dp").astype(jnp.float32),
        lax.psum(reduce_term.astype(jnp.bfloat16), "dp").astype(jnp.float32),
    )
    return (
        block_out,
        input_slope,
        gain_one_sum,
        shift_one_sum,
        gain_two_sum,
        shift_two_sum,
        triple_sum,
        triple_bias_sum,
        output_sum,
        bias_sum,
        expand_sum,
        expand_bias_sum,
        reduce_sum,
        bias_sum,
    )


TILE = 256
ROOM_FIRST = 62


def whole(memory_space=pltpu.VMEM):
    return pl.BlockSpec(memory_space=memory_space)


def local_call(kernel, outs, args, scratch=(), flops=0, room=8):
    size = lambda a: math.prod(a.shape) * jnp.dtype(a.dtype).itemsize
    moved = sum(size(a) for a in (*args, *outs))
    limit = moved + sum(size(a) for a in scratch) + room * 1024 * 1024
    limit = min(limit, 62 * 1024 * 1024)
    return pl.pallas_call(
        kernel,
        out_shape=tuple(outs),
        in_specs=[whole(pltpu.SMEM)] + [whole()] * (len(args) - 1),
        out_specs=tuple(whole() for _ in outs),
        scratch_shapes=list(scratch),
        cost_estimate=pl.CostEstimate(flops=flops, bytes_accessed=moved, transcendentals=0),
        compiler_params=pltpu.CompilerParams(vmem_limit_bytes=limit),
    )(*args)


def shape_of(*dims, dtype=jnp.bfloat16):
    return jax.ShapeDtypeStruct(dims, dtype)


def first_kernel(at, *refs):
    *six, bias, more, cotangent, segments, live, out, more_out, upstream = refs
    for index, ref in enumerate(six):
        out[index] = ref[...].astype(jnp.float32)
    for index in range(3):
        out[6 + index] = bias[index * out.shape[1] : (index + 1) * out.shape[1]].astype(jnp.float32)
    units = more_out.shape[1]
    for core in range(2):

        @pl.when(at[1] == core)
        def _(core=core):
            more_out[0] = more[core * units : (core + 1) * units].astype(jnp.float32)

    row, width = cotangent.shape
    alive = live[...].astype(jnp.float32).reshape(1, row)
    column = jnp.broadcast_to(alive, (row, row)).T[:, 0:1]
    upstream[:row] = (cotangent[...].astype(jnp.float32) * column).astype(jnp.bfloat16)
    ids = segments[...].astype(jnp.float32).reshape(1, row)
    slots = lax.broadcasted_iota(jnp.int32, (1, row), 1).astype(jnp.float32)
    keys = jnp.where(alive > 0, ids, -1.0 - slots)
    line = lax.broadcasted_iota(jnp.int32, (16, row), 0)
    marks = jnp.where(line == 0, ids, jnp.where(line == 1, keys, 0.0))
    upstream[row:, :row] = marks.astype(jnp.bfloat16)
    upstream[row:, row:] = jnp.zeros((16, width - row), jnp.bfloat16)


def vectors_kernel(at, own, got, bias, full, bias_mine):
    half = own.shape[1]
    for side in range(2):

        @pl.when(at[0] == side)
        def _(side=side):
            full[:, side * half : (side + 1) * half] = own[0:6]
            full[:, (1 - side) * half : (2 - side) * half] = got[0:6]
            for index in range(3):
                mine = (side * 3 + index) * half
                other = ((1 - side) * 3 + index) * half
                bias[0:1, mine : mine + half] = own[6 + index : 7 + index]
                bias[0:1, other : other + half] = got[6 + index : 7 + index]

    arrange(bias, bias_mine, at[0] * 2 + at[1])


def arrange(source, target, part):
    cols = target.shape[1] // 3
    for each in range(4):

        @pl.when(part == each)
        def _(each=each):
            for head in range(cols // HEAD):
                for kind in range(3):
                    start = kind * 4 * cols + each * cols + head * HEAD
                    to = head * 2 * HEAD + kind * HEAD if kind < 2 else 2 * cols + head * HEAD
                    target[:, to : to + HEAD] = source[:, start : start + HEAD]


def prepare_kernel(at, weight, out, *, other):
    arrange(weight, out, (at[0] * 2 + at[1]) ^ (2 if other else 0))


def feed_forward_kernel(at, *refs):
    count = (len(refs) - 4) // 7
    units = refs[-1].shape[1]
    my_units = pl.ds(pl.multiple_of(at[1] * units, 128), units)
    hiddens, (vectors, expand, expand_bias, reduce), outs = (
        refs[:count], refs[count : count + 4], refs[count + 4 :]
    )
    for index, hidden in enumerate(hiddens):
        act_one, act_two, normed_out, feed, slope, feed_hidden = outs[index * 6 : index * 6 + 6]
        normed, _ = normalize(hidden[...].astype(jnp.float32))
        normed_out[...] = normed.astype(jnp.bfloat16)
        act_one[...] = (normed * vectors[0:1] + vectors[1:2]).astype(jnp.bfloat16)
        two = (normed * vectors[2:3] + vectors[3:4]).astype(jnp.bfloat16)
        act_two[...] = two
        pre = product(two, expand[:, my_units]) + expand_bias[0:1]
        bell = 0.5 * (1.0 + lax.erf(pre * ROOT_HALF))
        out = (pre * bell).astype(jnp.bfloat16)
        feed_hidden[...] = out
        slope[...] = (bell + pre * DENSITY * jnp.exp(-0.5 * pre * pre)).astype(jnp.bfloat16)
        feed[...] = product(out, reduce[my_units]).astype(jnp.bfloat16)


def part_rows(at, grads, keep, send, parts):
    count, rows = keep.shape[0], keep.shape[1]
    most = rows // parts
    for piece in range(count):
        for each in range(parts):
            start = each * 2 * count * most + piece * most
            at_keep = pl.ds(pl.multiple_of(start + at[2] * count * most, 16), most)
            at_send = pl.ds(pl.multiple_of(start + (1 - at[2]) * count * most, 16), most)
            keep[piece, each * most : (each + 1) * most] = grads[at_keep]
            first = piece * rows + each * most
            send[first : first + most] = grads[at_send].astype(jnp.bfloat16)


def summed_product(lefts, rights):
    return sum(transposed_times(left, right) for left, right in zip(lefts, rights))


def reduce_gradient_kernel(at, *refs):
    lefts, rights, (keep, send, grads) = refs[:4], refs[4:8], refs[8:]
    row = lefts[0].shape[0]

    @pl.loop(0, rights[0].shape[1] // TILE)
    def _(step):
        cols = pl.ds(pl.multiple_of(step * TILE, TILE), TILE)
        grads[:, cols] = summed_product([r[...] for r in lefts], [r[:row, cols] for r in rights])

    part_rows(at, grads, keep, send, 1)


def feed_backward_kernel(at, *refs):
    acts, upstreams, normeds, slopes = (refs[4 * i : 4 * i + 4] for i in range(4))
    vectors, expand, reduce = refs[16:19]
    slope_parts, (sums, keep, send), pre_grads, grads = refs[19:23], refs[23:26], refs[26], refs[27]
    row, units = acts[0].shape[0], grads.shape[1]
    my_units = pl.ds(pl.multiple_of(at[1] * units, 128), units)
    sums[...] = jnp.zeros_like(sums)
    for index in range(4):
        pre_grad = times_transposed(upstreams[index][:row], reduce[my_units])
        pre_grad = pre_grad * slopes[index][...].astype(jnp.float32)
        rounded = pre_grad.astype(jnp.bfloat16)
        pre_grads[index * row : (index + 1) * row] = rounded
        back = times_transposed(rounded, expand[:, my_units])
        slope_parts[index][...] = (back * vectors[2:3]).astype(jnp.bfloat16)
        sums[0:1] += jnp.sum(back * normeds[index][...].astype(jnp.float32), axis=0, keepdims=True)
        sums[1:2] += jnp.sum(back, axis=0, keepdims=True)
        sums[2:3] += jnp.sum(pre_grad, axis=0, keepdims=True)

    @pl.loop(0, grads.shape[1] // TILE)
    def _(step):
        cols = pl.ds(pl.multiple_of(step * TILE, TILE), TILE)
        grads[:, cols] = summed_product(
            [r[...] for r in acts],
            [pre_grads[index * row : (index + 1) * row, cols] for index in range(4)],
        )

    part_rows(at, grads, keep, send, 1)


def attention_kernel(
    at, freqs, act_one, upstream, normed, feed, slope_part, vectors, mine, other, bias, output,
    both, context, triple_grads, sums, bias_sums,
):
    row, _ = act_one.shape
    half = mine.shape[0]
    cols = mine.shape[1] // 3
    heads = cols // HEAD
    score_scale = 1.0 / math.sqrt(HEAD)
    my_output = output[pl.ds(pl.multiple_of(at[1] * cols, 64), cols)]
    sums[...] = jnp.zeros_like(sums)
    bias_sums[...] = jnp.zeros_like(bias_sums)
    my_half = pl.ds(pl.multiple_of(at[0] * half, 128), half)
    other_half = pl.ds(pl.multiple_of((1 - at[0]) * half, 128), half)

    upper = lax.broadcasted_iota(jnp.int32, (row, row), 0)
    lower = lax.broadcasted_iota(jnp.int32, (row, row), 1)
    marks = upstream[row:, :row].astype(jnp.float32)
    key_row = jnp.broadcast_to(marks[1:2], (row, row))
    allowed = (key_row == key_row.T) & (lower <= upper)
    segment_row = jnp.broadcast_to(marks[0:1], (row, row))
    before = (segment_row == segment_row.T) & (upper < lower)
    position = jnp.sum(before.astype(jnp.float32), axis=0, keepdims=True)
    angle = freqs[:, 0:1] * position
    cosine, sine = jnp.cos(angle), jnp.sin(angle)
    none = jnp.zeros_like(sine)
    rest = jnp.zeros((HEAD - ROT, row), jnp.float32)
    cos = jnp.concatenate([cosine, cosine, rest + 1.0] * 2, axis=0).T
    low = jnp.concatenate([-sine, none, rest] * 2, axis=0).T
    high = jnp.concatenate([none, sine, rest] * 2, axis=0).T

    triple = product(act_one[:, my_half], mine[...]) + product(act_one[:, other_half], other[...])
    triple = triple + bias[...]
    context_grads = times_transposed(upstream[:row], my_output).astype(jnp.bfloat16)
    for head in range(heads):
        pair = triple[:, head * 2 * HEAD : (head + 1) * 2 * HEAD]
        turned = pair * cos + pltpu.roll(pair, 2 * HEAD - ROT // 2, 1) * low
        turned = (turned + pltpu.roll(pair, ROT // 2, 1) * high).astype(jnp.bfloat16)
        query, keys = turned[:, :HEAD], turned[:, HEAD:]
        at_head = slice(head * HEAD, (head + 1) * HEAD)
        at_pair = slice(head * 2 * HEAD, (head + 1) * 2 * HEAD)
        at_value = slice(2 * cols + head * HEAD, 2 * cols + (head + 1) * HEAD)
        values = triple[:, at_value].astype(jnp.bfloat16)
        scores = jnp.where(allowed, times_transposed(query, keys) * score_scale, NEGATIVE)
        top = jnp.max(scores, axis=-1, keepdims=True)
        weights = jnp.exp(scores - top)
        probs = weights * (1.0 / jnp.sum(weights, axis=-1, keepdims=True))
        probs_bf = probs.astype(jnp.bfloat16)
        context[:, at_head] = product(probs_bf, values).astype(jnp.bfloat16)
        context_grad = context_grads[:, at_head]
        value_grad = transposed_times(probs_bf, context_grad)
        prob_grad = times_transposed(context_grad, values)
        delta = jnp.sum(probs * prob_grad, axis=-1, keepdims=True)
        score_grad = (probs * (prob_grad - delta) * score_scale).astype(jnp.bfloat16)
        query_grad = product(score_grad, keys)
        key_grad = transposed_times(score_grad, query)
        grad = jnp.concatenate([query_grad, key_grad], axis=1)
        back = grad * cos - pltpu.roll(grad, 2 * HEAD - ROT // 2, 1) * low
        back = back - pltpu.roll(grad, ROT // 2, 1) * high
        triple_grads[:, at_pair] = back.astype(jnp.bfloat16)
        triple_grads[:, at_value] = value_grad.astype(jnp.bfloat16)
        bias_sums[0:1, at_pair] = jnp.sum(back, axis=0, keepdims=True)
        bias_sums[0:1, at_value] = jnp.sum(value_grad, axis=0, keepdims=True)

    total = product(context[...], my_output) + feed[...].astype(jnp.float32)
    both[0] = total.astype(both.dtype)
    for place, weight in ((my_half, mine), (other_half, other)):
        back = times_transposed(triple_grads[...], weight[...])
        sums[0:1, place] = jnp.sum(
            back * normed[:, place].astype(jnp.float32), axis=0, keepdims=True
        )
        sums[1:2, place] = jnp.sum(back, axis=0, keepdims=True)
        slope = back * vectors[0:1, place] + slope_part[:, place].astype(jnp.float32)
        both[1, :, place] = slope.astype(both.dtype)


def attention_gradient_kernel(at, *refs):
    acts, upstreams, contexts, triple_grads = (refs[4 * i : 4 * i + 4] for i in range(4))
    small, keep, send, small_out, grads = refs[16:]
    row, cols = contexts[0].shape

    @pl.loop(0, acts[0].shape[1] // TILE)
    def _(step):
        some = pl.ds(pl.multiple_of(step * TILE, TILE), TILE)
        grads[some, : 3 * cols] = summed_product(
            [r[:, some] for r in acts], [r[...] for r in triple_grads]
        )
        grads[some, 3 * cols :] = summed_product(
            [r[:row, some] for r in upstreams], [r[...] for r in contexts]
        )

    part_rows(at, grads, keep, send, 2)
    rounded = small[...].astype(jnp.bfloat16)
    small_out[...] = rounded
    send[keep.shape[0] * keep.shape[1] :] = rounded


def small_kernel(at, upstream, feed_sums, *refs):
    attend_sums, bias_sums, out = refs[:4], refs[4:8], refs[8]
    cols, row = bias_sums[0].shape[1], upstream.shape[0] - 16
    out[...] = jnp.zeros_like(out)
    out[0:2] = sum(ref[0:2] for ref in attend_sums)
    out[2:4] = feed_sums[0:2]
    out[4:5] = jnp.sum(upstream[:row].astype(jnp.float32), axis=0, keepdims=True)
    part = at[0] * 2 + at[1]
    out[pl.ds(5 + part, 1)] = feed_sums[2:3]
    out[pl.ds(9 + part, 1), :cols] = sum(ref[0:1] for ref in bias_sums)


def spread_small(at, small, outs, everywhere):
    *vectors, expand_bias, triple_bias = outs
    half = vectors[0].shape[0]
    units, cols = expand_bias.shape[0] // 2, triple_bias.shape[0] // 6
    for side in range(2):

        @pl.when(at[0] == side)
        def _(side=side):
            for index, vector in enumerate(vectors):
                vector[...] = small[min(index, 4), side * half : (side + 1) * half]
            for core in range(2):
                expand_bias[core * units : (core + 1) * units] = small[5 + side * 2 + core]

    for part in range(4):
        for head in range(cols // HEAD):
            for kind in range(3):
                start = head * 2 * HEAD + kind * HEAD if kind < 2 else 2 * cols + head * HEAD
                to = kind * 4 * cols + part * cols + head * HEAD
                everywhere[:, to : to + HEAD] = small[9 + part : 10 + part, start : start + HEAD]
    mine = pl.ds(pl.multiple_of(at[0] * 6 * cols, 128), 6 * cols)
    triple_bias[...] = everywhere[:, mine].reshape(6 * cols)


def theirs_kernel(at, kept, got, out):
    out[...] = (kept[...] + got[...].astype(jnp.float32)).astype(jnp.bfloat16)


def output_kernel(at, kept, got, got_across, hidden, upstream, vectors, block_out, input_slope):
    inputs = hidden[...].astype(jnp.float32)
    out, slope = (
        kept[i] + got[i].astype(jnp.float32) + got_across[i].astype(jnp.float32) for i in range(2)
    )
    block_out[...] = (inputs + out + vectors[4:5] + vectors[5:6]).astype(jnp.bfloat16)
    normed, scale = normalize(inputs)
    back = norm_back(slope, normed, scale, 1.0)
    input_slope[...] = upstream[: inputs.shape[0]].astype(jnp.float32) + back


def halve_kernel(at, keep, got, *refs, bit):
    *small, own, send = refs[: len(refs) // 2 + 1]
    small_out = refs[len(refs) // 2 + 1 :]
    count, rows = keep.shape[0], keep.shape[1]
    mine = (at[3] >> bit) & 1
    for each in range(count // 2):
        stay, leave = 2 * each + mine, 2 * each + 1 - mine
        theirs = got[pl.ds(pl.multiple_of(stay * rows, 16), rows)]
        own[each] = keep[stay] + theirs.astype(jnp.float32)
        theirs = got[pl.ds(pl.multiple_of(leave * rows, 16), rows)]
        total = keep[leave] + theirs.astype(jnp.float32)
        send[each * rows : (each + 1) * rows] = total.astype(jnp.bfloat16)
    if small:
        both = small[0][...].astype(jnp.float32) + got[count * rows :].astype(jnp.float32)
        both = both.astype(jnp.bfloat16)
        small_out[0][...] = both
        send[count // 2 * rows :] = both


def total_kernel(at, own, got, out):
    out[...] = (own[0] + got[...].astype(jnp.float32)).astype(jnp.bfloat16)


def swap_kernel(at, own, got, small, total, leave):
    rows, columns = total.shape[0] // 2, leave.shape[1] * 3 // 4
    total[...] = (own[0] + got[: 2 * rows].astype(jnp.float32)).astype(jnp.bfloat16)
    leave[:rows, :columns] = total[pl.ds(pl.multiple_of((1 - at[0]) * rows, 16), rows), :columns]
    leave[:rows, columns:] = jnp.zeros((rows, leave.shape[1] - columns), jnp.bfloat16)
    both = small[...].astype(jnp.float32) + got[2 * rows :].astype(jnp.float32)
    leave[rows:] = both.astype(jnp.bfloat16)


def merge_kernel(at, total, leave, got, out, small):
    rows = out.shape[0]
    columns = got.shape[1] * 3 // 4
    rest = total.shape[1] - columns
    for side in range(2):

        @pl.when(at[0] == side)
        def _(side=side):
            out[:, side * columns : (side + 1) * columns] = total[side * rows : (side + 1) * rows, :columns]
            out[:, (1 - side) * columns : (2 - side) * columns] = got[:rows, :columns]

    for side in range(2):
        start = 2 * columns + side * rest
        out[:, start : start + rest] = total[side * rows : (side + 1) * rows, columns:]
    both = leave[rows:].astype(jnp.float32) + got[rows:].astype(jnp.float32)
    small[...] = both.astype(jnp.bfloat16)


def join_kernel(at, *refs):
    *pieces, out = refs
    rows = pieces[0].shape[0]
    for step, piece in enumerate(pieces):
        out[pl.ds(pl.multiple_of((at[3] ^ step) * rows, 16), rows)] = piece[...]


def join_last_kernel(at, *refs):
    *pieces, small, out = refs
    join_kernel(at, *pieces, out)
    rows, width = len(pieces) * pieces[0].shape[0], small.shape[1]
    out[rows:, :width] = small[...]
    out[rows:, width:] = jnp.zeros((16, out.shape[1] - width), jnp.bfloat16)


def finish_rows_kernel(at, own, far, own_other, far_other, out):
    rows = own.shape[0]
    for core, pair in enumerate(((own, far), (own_other, far_other))):
        for side, piece in enumerate(pair):
            start = ((at[1] ^ core) * 2 + (at[2] ^ side)) * rows
            out[pl.ds(pl.multiple_of(start, 16), rows)] = piece[...].astype(jnp.float32)


def finish_columns_kernel(at, own, far, own_other, far_other, out):
    rows, cols = own.shape
    for core, pair in enumerate(((own, far), (own_other, far_other))):
        for side, piece in enumerate(pair):
            at_rows = pl.ds(pl.multiple_of((at[2] ^ side) * rows, 16), rows)
            at_cols = pl.ds(pl.multiple_of((at[1] ^ core) * cols, 128), cols)
            out[at_rows, at_cols] = piece[...].astype(jnp.float32)


def finish_attention_kernel(at, own, far, own_other, far_other, *refs):
    triple, output, *vectors = refs[:10]
    mine, other, small, everywhere = refs[10:]
    rows, half = own.shape[0], triple.shape[0]
    cols = triple.shape[1] // 12
    for target, pair in ((mine, (own, far)), (other, (own_other, far_other))):
        for side, piece in enumerate(pair):
            at_rows = pl.ds(pl.multiple_of((at[2] ^ side) * rows, 16), rows)
            target[at_rows] = piece[:rows]
    small[...] = far[rows:, : small.shape[1]].astype(jnp.float32) + far_other[
        rows:, : small.shape[1]
    ].astype(jnp.float32)
    spread_small(at, small, vectors, everywhere)

    def place(source, core):
        for side in range(2):
            part = side * 2 + core
            base = side * 3 * cols
            for head in range(cols // HEAD):
                for kind in range(3):
                    start = head * 2 * HEAD + kind * HEAD if kind < 2 else 2 * cols + head * HEAD
                    to = kind * 4 * cols + part * cols + head * HEAD
                    triple[:, to : to + HEAD] = source[:, base + start : base + start + HEAD].astype(
                        jnp.float32
                    )
            turned = source[:, 6 * cols + side * cols : 6 * cols + (side + 1) * cols]
            output[core * cols : (core + 1) * cols, side * half : (side + 1) * half] = turned.astype(
                jnp.float32
            ).T

    for core in range(2):

        @pl.when(at[1] == core)
        def _(core=core):
            place(mine, core)
            place(other, 1 - core)


def split_body(groups):
    depth = groups // 4

    def flip_dp(values, bits):
        return lax.ppermute(values, "dp", [(i, i ^ bits) for i in range(groups)])

    def flip_core(values):
        return flip_dp(values, 1)

    def flip_y(values):
        return flip_dp(values, 2)

    def flip_x(values):
        return lax.ppermute(values, "shard", [(0, 1), (1, 0)])

    def body(
        hidden_in,
        cotangent,
        segment_ids,
        live_mask,
        attend_gain,
        attend_shift,
        feed_gain,
        feed_shift,
        triple_weight,
        triple_bias,
        output_weight,
        output_bias,
        expand_weight,
        expand_bias,
        reduce_weight,
        reduce_bias,
    ):
        return layer(
            hidden_in, cotangent, segment_ids, live_mask,
            (attend_gain, attend_shift, feed_gain, feed_shift, output_bias, reduce_bias),
            triple_weight, triple_bias, output_weight, expand_weight, expand_bias, reduce_weight,
        )

    def layer(
        hidden_in, cotangent, segment_ids, live_mask, six_vectors,
        triple_weight, triple_bias, output_weight, expand_weight, expand_bias, reduce_weight,
    ):
        row, width = hidden_in.shape
        tokens = 4 * row
        side = lax.axis_index("shard")
        place = lax.axis_index("dp")
        core = place & 1
        at = jnp.stack([side, core, (place >> 1) & 1, place >> 2]).astype(jnp.int32)
        cols = triple_weight.shape[1] // 12
        units = expand_weight.shape[1] // 2
        half = width // 2
        f32 = jnp.float32

        def gather_rows(values):
            across = flip_x(values)
            return (values, flip_core(values), across, flip_core(across))

        packed, expand_bias_mine, upstream_own = local_call(
            first_kernel,
            [
                shape_of(16, half, dtype=f32),
                shape_of(8, units, dtype=f32),
                shape_of(row + 16, width),
            ],
            (at, *six_vectors, triple_bias, expand_bias, cotangent, segment_ids, live_mask),
            room=ROOM_FIRST,
        )
        packed_other = flip_x(packed)
        hidden = gather_rows(hidden_in)
        upstreams = gather_rows(upstream_own)
        _, full, bias = local_call(
            vectors_kernel,
            [
                shape_of(1, 12 * cols, dtype=f32),
                shape_of(6, width, dtype=f32),
                shape_of(1, 3 * cols, dtype=f32),
            ],
            (at, packed, packed_other),
        )
        freqs = 10000.0 ** (-np.arange(0, ROT, 2, dtype=np.float32) / ROT)
        freqs = jnp.asarray(np.broadcast_to(freqs[:, None], (ROT // 2, 128)).astype(np.float32))

        def prepare(other):
            return local_call(
                functools.partial(prepare_kernel, other=other),
                [shape_of(half, 3 * cols)],
                (at, triple_weight),
            )[0]

        triple_other = flip_x(prepare(True))
        triple_mine = prepare(False)

        piece_rows = half // depth
        keep_shape = shape_of(depth, piece_rows, width, dtype=f32)
        send_shape = shape_of(half, width)
        flops = 2 * tokens * width * units
        tiles = []
        for index in range(2):
            outs = local_call(
                feed_forward_kernel,
                [shape_of(row, width)] * 12,
                (
                    at, *hidden[2 * index : 2 * index + 2], full, expand_weight,
                    expand_bias_mine, reduce_weight,
                ),
                flops=flops,
            )
            tiles += [outs[:6], outs[6:]]
        act_ones, act_twos, normeds, feeds, slopes, feed_hiddens = zip(*tiles)
        reduce_parts = local_call(
            reduce_gradient_kernel,
            [keep_shape, send_shape],
            (at, *feed_hiddens, *upstreams),
            [pltpu.VMEM((units, width), f32)],
            flops,
        )
        *slope_parts, feed_sums, keep, send = local_call(
            feed_backward_kernel,
            [shape_of(row, width)] * 4 + [shape_of(8, width, dtype=f32), keep_shape, send_shape],
            (at, *act_twos, *upstreams, *normeds, *slopes, full, expand_weight, reduce_weight),
            [pltpu.VMEM((tokens, units), jnp.bfloat16), pltpu.VMEM((width, units), f32)],
            3 * flops,
        )
        expand_parts = keep, send
        attended = [None] * 4
        for index in (1, 3, 0, 2):
            kind = jnp.bfloat16 if index % 2 else f32
            attended[index] = local_call(
                attention_kernel,
                [
                    shape_of(2, row, width, dtype=kind),
                    shape_of(row, cols),
                    shape_of(row, 3 * cols),
                    shape_of(8, width, dtype=f32),
                    shape_of(8, 3 * cols, dtype=f32),
                ],
                (
                    at, freqs, act_ones[index], upstreams[index], normeds[index],
                    feeds[index], slope_parts[index], full, triple_mine, triple_other, bias,
                    output_weight,
                ),
                flops=flops,
            )
        boths, contexts, triple_grads, attend_sums, bias_sums = zip(*attended)
        (small,) = local_call(
            small_kernel,
            [shape_of(16, width, dtype=f32)],
            (at, upstream_own, feed_sums, *attend_sums, *bias_sums),
            room=2,
        )
        triple_parts = local_call(
            attention_gradient_kernel,
            [keep_shape, shape_of(half + 16, width), shape_of(16, width)],
            (at, *act_ones, *upstreams, *contexts, *triple_grads, small),
            [pltpu.VMEM((width, 4 * cols), f32)],
            flops,
        )

        (theirs,) = local_call(
            theirs_kernel, [shape_of(2, row, width)], (at, boths[2], flip_core(boths[3])), room=2
        )
        block_out, input_slope = local_call(
            output_kernel,
            [shape_of(row, width), shape_of(row, width, dtype=f32)],
            (
                at, boths[0], flip_core(boths[1]), flip_x(theirs), hidden_in,
                upstream_own, full,
            ),
            room=6,
        )

        def reduce_pieces(keep, send, *small):
            got, count, extra = flip_y(send), depth, 16 * len(small)
            for bit in range(depth.bit_length() - 1):
                count //= 2
                keep, send, *small = local_call(
                    functools.partial(halve_kernel, bit=bit),
                    [
                        shape_of(count, piece_rows, width, dtype=f32),
                        shape_of(count * piece_rows + extra, width),
                    ]
                    + [shape_of(16, width)] * len(small),
                    (at, keep, got, *small),
                    room=2,
                )
                got = flip_dp(send, 4 << bit)
            piece = shape_of(piece_rows, width)
            if not small:
                return local_call(total_kernel, [piece], (at, keep, got), room=2)
            rows = piece_rows // 2
            total, leave = local_call(
                swap_kernel, [piece, shape_of(rows + 16, width)], (at, keep, got, *small), room=2
            )
            return local_call(
                merge_kernel,
                [shape_of(rows, 2 * width), shape_of(16, width)],
                (at, total, leave, flip_x(leave)),
                room=2,
            )

        def gather_pieces(piece, *more):
            pieces, step = [piece] + [None] * (depth - 1), depth
            while step > 1:
                step //= 2
                for at_piece in range(step, depth, 2 * step):
                    near = pieces[at_piece - step]
                    pieces[at_piece] = flip_dp(near, 4 * step)
            rows, cols = depth * piece.shape[0], piece.shape[1]
            (own,) = local_call(join_kernel, [shape_of(rows, cols)], (at, *pieces), room=2)
            own_other = flip_core(own)
            if more:
                far = [flip_y(each) for each in pieces]
                (far,) = local_call(
                    join_last_kernel, [shape_of(rows + 16, cols)], (at, *far, *more), room=2
                )
            else:
                far = flip_y(own)
            return at, own, far, own_other, flip_core(far)

        (reduce_sum,) = local_call(
            finish_rows_kernel,
            [shape_of(2 * units, width, dtype=f32)],
            gather_pieces(*reduce_pieces(*reduce_parts)),
            room=2,
        )
        (expand_sum,) = local_call(
            finish_columns_kernel,
            [shape_of(width, 2 * units, dtype=f32)],
            gather_pieces(*reduce_pieces(*expand_parts)),
            room=2,
        )
        vector = shape_of(half, dtype=f32)
        triple_sum, output_sum, *vectors, bias_sum, bias_again, expand_bias_sum, triple_bias_sum = local_call(
            finish_attention_kernel,
            [shape_of(half, 12 * cols, dtype=f32), shape_of(2 * cols, width, dtype=f32)]
            + [vector] * 6
            + [shape_of(2 * units, dtype=f32), shape_of(6 * cols, dtype=f32)],
            gather_pieces(*reduce_pieces(*triple_parts)),
            [
                pltpu.VMEM((half, 2 * width), jnp.bfloat16),
                pltpu.VMEM((half, 2 * width), jnp.bfloat16),
                pltpu.VMEM((16, width), f32),
                pltpu.VMEM((1, 12 * cols), f32),
            ],
            room=4,
        )
        return (
            block_out,
            input_slope,
            *vectors,
            triple_sum,
            triple_bias_sum,
            output_sum,
            bias_sum,
            expand_sum,
            expand_bias_sum,
            reduce_sum,
            bias_again,
        )

    return body


def solution(mesh):
    placed = (
        P(("dp", "shard"), None),
        P(("dp", "shard"), None),
        P(("dp", "shard")),
        P(("dp", "shard")),
        P("shard"),
        P("shard"),
        P("shard"),
        P("shard"),
        P("shard", None),
        P("shard"),
        P("shard", None),
        P("shard"),
        P(None, "shard"),
        P("shard"),
        P("shard", None),
        P("shard"),
    )
    split = mesh.shape['shard'] == 2 and HEADS % 4 == 0
    whole_rows = mesh.shape['dp'] >= 8 and mesh.shape['dp'] & (mesh.shape['dp'] - 1) == 0
    split = split and whole_rows
    body = split_body(mesh.shape['dp']) if split else gathered_body
    return jax.shard_map(
        body,
        mesh=mesh,
        in_specs=placed,
        out_specs=(
            P(("dp", "shard"), None),
            P(("dp", "shard"), None),
            P("shard"),
            P("shard"),
            P("shard"),
            P("shard"),
            P("shard", None),
            P("shard"),
            P("shard", None),
            P("shard"),
            P(None, "shard"),
            P("shard"),
            P("shard", None),
            P("shard"),
        ),
        check_vma=False,
    )
```

```python
import functools
import math

import jax
import jax.numpy as jnp
import numpy as np
from jax import lax
from jax.experimental import pallas as pl
from jax.experimental.pallas import tpu as pltpu
from jax.sharding import PartitionSpec as P


HEADS = 12
HEAD = 64
ROT = 16


EPSILON = 1e-05
ROOT_HALF = 0.7071067811865476
DENSITY = 0.3989422804014327
NEGATIVE = -1e30


def product(left, right):
    return jnp.dot(left, right, preferred_element_type=jnp.float32)


def times_transposed(left, right):
    return lax.dot_general(
        left, right, (((1,), (1,)), ((), ())), preferred_element_type=jnp.float32
    )


def transposed_times(left, right):
    return lax.dot_general(
        left, right, (((0,), (0,)), ((), ())), preferred_element_type=jnp.float32
    )


def normalize(values):
    mean = jnp.mean(values, axis=-1, keepdims=True)
    centered = values - mean
    spread = jnp.mean(centered * centered, axis=-1, keepdims=True)
    scale = lax.rsqrt(spread + EPSILON)
    return (centered * scale, scale)


def norm_back(grad_out, normed, scale, gain):
    scaled = grad_out * gain
    first = jnp.mean(scaled, axis=-1, keepdims=True)
    second = jnp.mean(scaled * normed, axis=-1, keepdims=True)
    return scale * (scaled - first - normed * second)


def smooth_gate(values):
    return 0.5 * values * (1.0 + lax.erf(values * ROOT_HALF))


def smooth_slope(values):
    return 0.5 * (1.0 + lax.erf(values * ROOT_HALF)) + values * DENSITY * jnp.exp(
        -0.5 * values * values
    )


def rotary_tables(segment_row):
    count = segment_row.shape[0]
    index = jnp.arange(count)
    same = segment_row[:, None] == segment_row[None, :]
    before = index[None, :] < index[:, None]
    position = jnp.sum((same & before).astype(jnp.float32), axis=1)
    freqs = jnp.power(10000.0, -jnp.arange(0, ROT, 2).astype(jnp.float32) / ROT)
    angle = position[:, None] * freqs[None, :]
    angle = jnp.concatenate([angle, angle], axis=1)
    return (jnp.cos(angle), jnp.sin(angle))


def allowed_mask(segment_row, live_row):
    count = segment_row.shape[0]
    index = jnp.arange(count)
    same = segment_row[:, None] == segment_row[None, :]
    causal = index[None, :] <= index[:, None]
    both = (live_row[:, None] > 0) & (live_row[None, :] > 0)
    diagonal = index[:, None] == index[None, :]
    return same & causal & (both | diagonal)


def rotate(heads, cosine, sine):
    half = ROT // 2
    part = heads[..., :ROT]
    turned = jnp.concatenate([-part[..., half:], part[..., :half]], axis=-1)
    mixed = part * jnp.expand_dims(cosine, -2) + turned * jnp.expand_dims(sine, -2)
    return jnp.concatenate([mixed, heads[..., ROT:]], axis=-1)


def rotate_back(grads, cosine, sine):
    half = ROT // 2
    part = grads[..., :ROT]
    sined = part * jnp.expand_dims(sine, -2)
    turned = jnp.concatenate([sined[..., half:], -sined[..., :half]], axis=-1)
    mixed = part * jnp.expand_dims(cosine, -2) + turned
    return jnp.concatenate([mixed, grads[..., ROT:]], axis=-1)


def masked_scores(query, keys, allowed):
    scale = 1.0 / math.sqrt(HEAD)
    scores = jnp.einsum("qhd,khd->hqk", query, keys, preferred_element_type=jnp.float32) * scale
    return jnp.where(allowed[None], scores, NEGATIVE)


def attend(query, keys, values, allowed):
    scores = masked_scores(query, keys, allowed)
    top = jnp.max(scores, axis=-1, keepdims=True)
    total = jnp.sum(jnp.exp(scores - top), axis=-1, keepdims=True)
    logsum = top + jnp.log(total)
    probs = jnp.exp(scores - logsum).astype(jnp.bfloat16)
    context = jnp.einsum("hqk,khd->qhd", probs, values, preferred_element_type=jnp.float32)
    return (context.astype(jnp.bfloat16), logsum)


def attend_back(query, keys, values, allowed, logsum, context_grad):
    scale = 1.0 / math.sqrt(HEAD)
    probs = jnp.exp(masked_scores(query, keys, allowed) - logsum)
    probs_bf = probs.astype(jnp.bfloat16)
    value_grad = jnp.einsum(
        "hqk,qhd->khd", probs_bf, context_grad, preferred_element_type=jnp.float32
    )
    prob_grad = jnp.einsum("qhd,khd->hqk", context_grad, values, preferred_element_type=jnp.float32)
    delta = jnp.sum(probs * prob_grad, axis=-1, keepdims=True)
    score_grad = (probs * (prob_grad - delta) * scale).astype(jnp.bfloat16)
    query_grad = jnp.einsum("hqk,khd->qhd", score_grad, keys, preferred_element_type=jnp.float32)
    key_grad = jnp.einsum("hqk,qhd->khd", score_grad, query, preferred_element_type=jnp.float32)
    return (query_grad, key_grad, value_grad)


def gathered_body(
    hidden_in,
    cotangent,
    segment_ids,
    live_mask,
    attend_gain,
    attend_shift,
    feed_gain,
    feed_shift,
    triple_weight,
    triple_bias,
    output_weight,
    output_bias,
    expand_weight,
    expand_bias,
    reduce_weight,
    reduce_bias,
):
    tokens = hidden_in.shape[0]
    width = HEADS * HEAD
    shaped = (tokens, HEADS, HEAD)
    (
        gain_one,
        shift_one,
        gain_two,
        shift_two,
        triple_full,
        triple_bias_full,
        output_full,
        output_bias_full,
        reduce_bias_full,
    ) = (
        lax.all_gather(attend_gain, "shard", axis=0, tiled=True),
        lax.all_gather(attend_shift, "shard", axis=0, tiled=True),
        lax.all_gather(feed_gain, "shard", axis=0, tiled=True),
        lax.all_gather(feed_shift, "shard", axis=0, tiled=True),
        lax.all_gather(triple_weight, "shard", axis=0, tiled=True),
        lax.all_gather(triple_bias, "shard", axis=0, tiled=True),
        lax.all_gather(output_weight, "shard", axis=0, tiled=True),
        lax.all_gather(output_bias, "shard", axis=0, tiled=True),
        lax.all_gather(reduce_bias, "shard", axis=0, tiled=True),
    )
    inputs32 = hidden_in.astype(jnp.float32)
    normed, scale = normalize(inputs32)
    act_one = (normed * gain_one.astype(jnp.float32) + shift_one.astype(jnp.float32)).astype(
        jnp.bfloat16
    )
    act_two = (normed * gain_two.astype(jnp.float32) + shift_two.astype(jnp.float32)).astype(
        jnp.bfloat16
    )
    cosine, sine = rotary_tables(segment_ids)
    allowed = allowed_mask(segment_ids, live_mask)
    triple = product(act_one, triple_full) + triple_bias_full.astype(jnp.float32)
    query = rotate(triple[:, :width].reshape(shaped), cosine, sine).astype(jnp.bfloat16)
    keys = rotate(triple[:, width : 2 * width].reshape(shaped), cosine, sine).astype(jnp.bfloat16)
    values = triple[:, 2 * width :].reshape(shaped).astype(jnp.bfloat16)
    context, logsum = attend(query, keys, values, allowed)
    context_flat = context.reshape(tokens, width)
    attention = product(context_flat, output_full) + output_bias_full.astype(jnp.float32)
    expand_full, expand_bias_full, reduce_full = (
        lax.all_gather(expand_weight, "shard", axis=1, tiled=True),
        lax.all_gather(expand_bias, "shard", axis=0, tiled=True),
        lax.all_gather(reduce_weight, "shard", axis=0, tiled=True),
    )
    feed_pre = product(act_two, expand_full) + expand_bias_full.astype(jnp.float32)
    feed_hidden = smooth_gate(feed_pre).astype(jnp.bfloat16)
    feed = product(feed_hidden, reduce_full)
    block_out = (inputs32 + attention + feed + reduce_bias_full.astype(jnp.float32)).astype(
        jnp.bfloat16
    )
    upstream = cotangent.astype(jnp.float32) * live_mask.astype(jnp.float32)[:, None]
    upstream_bf = upstream.astype(jnp.bfloat16)
    gain_one_again, gain_two_again, triple_again, output_again = (
        lax.all_gather(attend_gain, "shard", axis=0, tiled=True),
        lax.all_gather(feed_gain, "shard", axis=0, tiled=True),
        lax.all_gather(triple_weight, "shard", axis=0, tiled=True),
        lax.all_gather(output_weight, "shard", axis=0, tiled=True),
    )
    expand_again, reduce_again = (
        lax.all_gather(expand_weight, "shard", axis=1, tiled=True),
        lax.all_gather(reduce_weight, "shard", axis=0, tiled=True),
    )
    pre_grad = times_transposed(upstream_bf, reduce_again) * smooth_slope(feed_pre)
    pre_grad_bf = pre_grad.astype(jnp.bfloat16)
    feed_input_grad = times_transposed(pre_grad_bf, expand_again)
    expand_term, expand_bias_term, reduce_term = (
        lax.psum_scatter(
            transposed_times(act_two, pre_grad_bf).astype(jnp.bfloat16),
            "shard",
            scatter_dimension=1,
            tiled=True,
        ).astype(jnp.float32),
        lax.psum_scatter(
            jnp.sum(pre_grad, axis=0).astype(jnp.bfloat16), "shard", scatter_dimension=0, tiled=True
        ).astype(jnp.float32),
        lax.psum_scatter(
            transposed_times(feed_hidden, upstream_bf).astype(jnp.bfloat16),
            "shard",
            scatter_dimension=0,
            tiled=True,
        ).astype(jnp.float32),
    )
    bias_term = jnp.sum(upstream, axis=0)
    output_term = transposed_times(context_flat, upstream_bf)
    context_grad = times_transposed(upstream_bf, output_again).astype(jnp.bfloat16).reshape(shaped)
    query_grad, key_grad, value_grad = attend_back(
        query, keys, values, allowed, logsum, context_grad
    )
    triple_grad = jnp.concatenate(
        [
            rotate_back(query_grad, cosine, sine).reshape(tokens, width),
            rotate_back(key_grad, cosine, sine).reshape(tokens, width),
            value_grad.reshape(tokens, width),
        ],
        axis=1,
    )
    triple_bias_term = jnp.sum(triple_grad, axis=0)
    triple_grad_bf = triple_grad.astype(jnp.bfloat16)
    triple_term = transposed_times(act_one, triple_grad_bf)
    attend_input_grad = times_transposed(triple_grad_bf, triple_again)
    gain_one_term = jnp.sum(attend_input_grad * normed, axis=0)
    shift_one_term = jnp.sum(attend_input_grad, axis=0)
    gain_two_term = jnp.sum(feed_input_grad * normed, axis=0)
    shift_two_term = jnp.sum(feed_input_grad, axis=0)
    input_slope = (
        upstream
        + norm_back(attend_input_grad, normed, scale, gain_one_again.astype(jnp.float32))
        + norm_back(feed_input_grad, normed, scale, gain_two_again.astype(jnp.float32))
    )
    (
        gain_one_part,
        shift_one_part,
        gain_two_part,
        shift_two_part,
        triple_part,
        triple_bias_part,
        output_part,
        bias_part,
    ) = (
        lax.psum_scatter(
            gain_one_term.astype(jnp.bfloat16), "shard", scatter_dimension=0, tiled=True
        ).astype(jnp.float32),
        lax.psum_scatter(
            shift_one_term.astype(jnp.bfloat16), "shard", scatter_dimension=0, tiled=True
        ).astype(jnp.float32),
        lax.psum_scatter(
            gain_two_term.astype(jnp.bfloat16), "shard", scatter_dimension=0, tiled=True
        ).astype(jnp.float32),
        lax.psum_scatter(
            shift_two_term.astype(jnp.bfloat16), "shard", scatter_dimension=0, tiled=True
        ).astype(jnp.float32),
        lax.psum_scatter(
            triple_term.astype(jnp.bfloat16), "shard", scatter_dimension=0, tiled=True
        ).astype(jnp.float32),
        lax.psum_scatter(
            triple_bias_term.astype(jnp.bfloat16), "shard", scatter_dimension=0, tiled=True
        ).astype(jnp.float32),
        lax.psum_scatter(
            output_term.astype(jnp.bfloat16), "shard", scatter_dimension=0, tiled=True
        ).astype(jnp.float32),
        lax.psum_scatter(
            bias_term.astype(jnp.bfloat16), "shard", scatter_dimension=0, tiled=True
        ).astype(jnp.float32),
    )
    (
        gain_one_sum,
        shift_one_sum,
        gain_two_sum,
        shift_two_sum,
        triple_sum,
        triple_bias_sum,
        output_sum,
        bias_sum,
        expand_sum,
        expand_bias_sum,
        reduce_sum,
    ) = (
        lax.psum(gain_one_part.astype(jnp.bfloat16), "dp").astype(jnp.float32),
        lax.psum(shift_one_part.astype(jnp.bfloat16), "dp").astype(jnp.float32),
        lax.psum(gain_two_part.astype(jnp.bfloat16), "dp").astype(jnp.float32),
        lax.psum(shift_two_part.astype(jnp.bfloat16), "dp").astype(jnp.float32),
        lax.psum(triple_part.astype(jnp.bfloat16), "dp").astype(jnp.float32),
        lax.psum(triple_bias_part.astype(jnp.bfloat16), "dp").astype(jnp.float32),
        lax.psum(output_part.astype(jnp.bfloat16), "dp").astype(jnp.float32),
        lax.psum(bias_part.astype(jnp.bfloat16), "dp").astype(jnp.float32),
        lax.psum(expand_term.astype(jnp.bfloat16), "dp").astype(jnp.float32),
        lax.psum(expand_bias_term.astype(jnp.bfloat16), "dp").astype(jnp.float32),
        lax.psum(reduce_term.astype(jnp.bfloat16), "dp").astype(jnp.float32),
    )
    return (
        block_out,
        input_slope,
        gain_one_sum,
        shift_one_sum,
        gain_two_sum,
        shift_two_sum,
        triple_sum,
        triple_bias_sum,
        output_sum,
        bias_sum,
        expand_sum,
        expand_bias_sum,
        reduce_sum,
        bias_sum,
    )


TILE = 256


def whole(memory_space=pltpu.VMEM):
    return pl.BlockSpec(memory_space=memory_space)


def local_call(kernel, outs, args, scratch=(), flops=0, room=8, space=pltpu.VMEM, hbm_out=False, alias=None):
    size = lambda a: math.prod(a.shape) * jnp.dtype(a.dtype).itemsize
    moved = sum(size(a) for a in (*args, *outs))
    limit = moved + sum(size(a) for a in scratch if "sem" not in str(a.dtype)) + room * 1024 * 1024
    limit = min(limit, 62 * 1024 * 1024)
    return pl.pallas_call(
        kernel,
        out_shape=tuple(outs),
        in_specs=[whole(pltpu.SMEM)]
        + [whole(pltpu.HBM if i == alias else space) for i in range(1, len(args))],
        out_specs=tuple(
            whole(pltpu.HBM if hbm_out and i == 0 else pltpu.VMEM) for i in range(len(outs))
        ),
        input_output_aliases={} if alias is None else {alias: 0},
        scratch_shapes=list(scratch),
        cost_estimate=pl.CostEstimate(flops=flops, bytes_accessed=moved, transcendentals=0),
        compiler_params=pltpu.CompilerParams(vmem_limit_bytes=limit),
    )(*args)


def shape_of(*dims, dtype=jnp.bfloat16):
    return jax.ShapeDtypeStruct(dims, dtype)


def first_kernel(at, *refs):
    given, (out, more_out, upstream), held, sems = refs[:11], refs[11:14], refs[14:25], refs[25]
    copies = [pltpu.make_async_copy(a, b, sems.at[i]) for i, (a, b) in enumerate(zip(given, held))]
    for copy in copies:
        copy.start()
    for copy in copies:
        copy.wait()
    *six, bias, more, cotangent, segments, live = held
    for index, ref in enumerate(six):
        out[index] = ref[...].astype(jnp.float32)
    for index in range(3):
        out[6 + index] = bias[index * out.shape[1] : (index + 1) * out.shape[1]].astype(jnp.float32)
    units = more_out.shape[1]
    for core in range(2):

        @pl.when(at[1] == core)
        def _(core=core):
            more_out[0] = more[core * units : (core + 1) * units].astype(jnp.float32)

    row, width = cotangent.shape
    alive = live[...].astype(jnp.float32).reshape(1, row)
    column = jnp.broadcast_to(alive, (row, row)).T[:, 0:1]
    upstream[:row] = (cotangent[...].astype(jnp.float32) * column).astype(jnp.bfloat16)
    ids = segments[...].astype(jnp.float32).reshape(1, row)
    slots = lax.broadcasted_iota(jnp.int32, (1, row), 1).astype(jnp.float32)
    keys = jnp.where(alive > 0, ids, -1.0 - slots)
    line = lax.broadcasted_iota(jnp.int32, (16, row), 0)
    marks = jnp.where(line == 0, ids, jnp.where(line == 1, keys, 0.0))
    upstream[row:, :row] = marks.astype(jnp.bfloat16)
    upstream[row:, row:] = jnp.zeros((16, width - row), jnp.bfloat16)


def vectors_kernel(at, own, got, bias, full, bias_mine):
    half = own.shape[1]
    for side in range(2):

        @pl.when(at[0] == side)
        def _(side=side):
            full[:, side * half : (side + 1) * half] = own[0:6]
            full[:, (1 - side) * half : (2 - side) * half] = got[0:6]
            for index in range(3):
                mine = (side * 3 + index) * half
                other = ((1 - side) * 3 + index) * half
                bias[0:1, mine : mine + half] = own[6 + index : 7 + index]
                bias[0:1, other : other + half] = got[6 + index : 7 + index]

    arrange(bias, bias_mine, at[0] * 2 + at[1])


def arrange(source, target, part):
    cols = target.shape[1] // 3
    for each in range(4):

        @pl.when(part == each)
        def _(each=each):
            for head in range(cols // HEAD):
                for kind in range(3):
                    start = kind * 4 * cols + each * cols + head * HEAD
                    to = head * 2 * HEAD + kind * HEAD if kind < 2 else 2 * cols + head * HEAD
                    target[:, to : to + HEAD] = source[:, start : start + HEAD]


def weights_kernel(
    at, triple, expand, reduce, output, mine, other, my_expand, my_reduce, my_output, held, sems
):
    units, cols = my_expand.shape[1], my_output.shape[0]
    my_units = pl.ds(pl.multiple_of(at[1] * units, 128), units)
    my_cols = pl.ds(pl.multiple_of(at[1] * cols, 16), cols)
    copies = [
        pltpu.make_async_copy(triple, held, sems.at[0]),
        pltpu.make_async_copy(expand.at[:, my_units], my_expand, sems.at[1]),
        pltpu.make_async_copy(reduce.at[my_units], my_reduce, sems.at[2]),
        pltpu.make_async_copy(output.at[my_cols], my_output, sems.at[3]),
    ]
    for copy in copies:
        copy.start()
    copies[0].wait()
    arrange(held, other, (at[0] * 2 + at[1]) ^ 2)
    arrange(held, mine, at[0] * 2 + at[1])
    for copy in copies[1:]:
        copy.wait()


def feed_forward_kernel(at, *refs):
    count = (len(refs) - 4) // 7
    hiddens, (vectors, expand, expand_bias, reduce), outs = (
        refs[:count], refs[count : count + 4], refs[count + 4 :]
    )
    for index, hidden in enumerate(hiddens):
        act_one, act_two, normed_out, feed, slope, feed_hidden = outs[index * 6 : index * 6 + 6]
        normed, _ = normalize(hidden[...].astype(jnp.float32))
        normed_out[...] = normed.astype(jnp.bfloat16)
        act_one[...] = (normed * vectors[0:1] + vectors[1:2]).astype(jnp.bfloat16)
        two = (normed * vectors[2:3] + vectors[3:4]).astype(jnp.bfloat16)
        act_two[...] = two
        pre = product(two, expand[...]) + expand_bias[0:1]
        bell = 0.5 * (1.0 + lax.erf(pre * ROOT_HALF))
        out = (pre * bell).astype(jnp.bfloat16)
        feed_hidden[...] = out
        slope[...] = (bell + pre * DENSITY * jnp.exp(-0.5 * pre * pre)).astype(jnp.bfloat16)
        feed[...] = product(out, reduce[...]).astype(jnp.bfloat16)


def part_rows(at, grads, keep, send, parts):
    count, rows = keep.shape[0], keep.shape[1]
    most = rows // parts
    for piece in range(count):
        for each in range(parts):
            start = each * 2 * count * most + piece * most
            at_keep = pl.ds(pl.multiple_of(start + at[2] * count * most, 16), most)
            at_send = pl.ds(pl.multiple_of(start + (1 - at[2]) * count * most, 16), most)
            keep[piece, each * most : (each + 1) * most] = grads[at_keep]
            first = piece * rows + each * most
            send[first : first + most] = grads[at_send].astype(jnp.bfloat16)


def summed_product(lefts, rights):
    return sum(transposed_times(left, right) for left, right in zip(lefts, rights))


def reduce_gradient_kernel(at, *refs):
    lefts, rights, (keep, send, grads) = refs[:4], refs[4:8], refs[8:]
    row = lefts[0].shape[0]

    @pl.loop(0, rights[0].shape[1] // TILE)
    def _(step):
        cols = pl.ds(pl.multiple_of(step * TILE, TILE), TILE)
        grads[:, cols] = summed_product([r[...] for r in lefts], [r[:row, cols] for r in rights])

    part_rows(at, grads, keep, send, 1)


def feed_backward_kernel(at, *refs):
    acts, upstreams, normeds, slopes = (refs[4 * i : 4 * i + 4] for i in range(4))
    vectors, expand, reduce = refs[16:19]
    slope_parts, (sums, keep, send), pre_grads, grads = refs[19:23], refs[23:26], refs[26], refs[27]
    row = acts[0].shape[0]
    sums[...] = jnp.zeros_like(sums)
    for index in range(4):
        pre_grad = times_transposed(upstreams[index][:row], reduce[...])
        pre_grad = pre_grad * slopes[index][...].astype(jnp.float32)
        rounded = pre_grad.astype(jnp.bfloat16)
        pre_grads[index * row : (index + 1) * row] = rounded
        back = times_transposed(rounded, expand[...])
        slope_parts[index][...] = (back * vectors[2:3]).astype(jnp.bfloat16)
        sums[0:1] += jnp.sum(back * normeds[index][...].astype(jnp.float32), axis=0, keepdims=True)
        sums[1:2] += jnp.sum(back, axis=0, keepdims=True)
        sums[2:3] += jnp.sum(pre_grad, axis=0, keepdims=True)

    @pl.loop(0, grads.shape[1] // TILE)
    def _(step):
        cols = pl.ds(pl.multiple_of(step * TILE, TILE), TILE)
        grads[:, cols] = summed_product(
            [r[...] for r in acts],
            [pre_grads[index * row : (index + 1) * row, cols] for index in range(4)],
        )

    part_rows(at, grads, keep, send, 1)


def attention_kernel(
    at, freqs, act_one, upstream, normed, feed, slope_part, vectors, mine, other, bias, output,
    both, context, triple_grads, sums, bias_sums,
):
    row, _ = act_one.shape
    half = mine.shape[0]
    cols = mine.shape[1] // 3
    heads = cols // HEAD
    score_scale = 1.0 / math.sqrt(HEAD)
    sums[...] = jnp.zeros_like(sums)
    bias_sums[...] = jnp.zeros_like(bias_sums)
    my_half = pl.ds(pl.multiple_of(at[0] * half, 128), half)
    other_half = pl.ds(pl.multiple_of((1 - at[0]) * half, 128), half)

    upper = lax.broadcasted_iota(jnp.int32, (row, row), 0)
    lower = lax.broadcasted_iota(jnp.int32, (row, row), 1)
    marks = upstream[row:, :row].astype(jnp.float32)
    key_row = jnp.broadcast_to(marks[1:2], (row, row))
    allowed = (key_row == key_row.T) & (lower <= upper)
    segment_row = jnp.broadcast_to(marks[0:1], (row, row))
    before = (segment_row == segment_row.T) & (upper < lower)
    position = jnp.sum(before.astype(jnp.float32), axis=0, keepdims=True)
    angle = freqs[:, 0:1] * position
    cosine, sine = jnp.cos(angle), jnp.sin(angle)
    none = jnp.zeros_like(sine)
    rest = jnp.zeros((HEAD - ROT, row), jnp.float32)
    cos = jnp.concatenate([cosine, cosine, rest + 1.0] * 2, axis=0).T
    low = jnp.concatenate([-sine, none, rest] * 2, axis=0).T
    high = jnp.concatenate([none, sine, rest] * 2, axis=0).T

    triple = product(act_one[:, my_half], mine[...]) + product(act_one[:, other_half], other[...])
    triple = triple + bias[...]
    context_grads = times_transposed(upstream[:row], output[...]).astype(jnp.bfloat16)
    each_head = range(heads)
    at_head = [slice(head * HEAD, (head + 1) * HEAD) for head in each_head]
    at_pair = [slice(head * 2 * HEAD, (head + 1) * 2 * HEAD) for head in each_head]
    at_value = [slice(2 * cols + head * HEAD, 2 * cols + (head + 1) * HEAD) for head in each_head]

    def turn(pair):
        turned = pair * cos + pltpu.roll(pair, 2 * HEAD - ROT // 2, 1) * low
        return (turned + pltpu.roll(pair, ROT // 2, 1) * high).astype(jnp.bfloat16)

    turned = [turn(triple[:, at_pair[head]]) for head in each_head]
    queries, keys = [t[:, :HEAD] for t in turned], [t[:, HEAD:] for t in turned]
    values = [triple[:, at_value[head]].astype(jnp.bfloat16) for head in each_head]
    context_grad = [context_grads[:, at_head[head]] for head in each_head]
    scores = [times_transposed(queries[head], keys[head]) for head in each_head]
    prob_grads = [times_transposed(context_grad[head], values[head]) for head in each_head]
    probs = []
    for head in each_head:
        masked = jnp.where(allowed, scores[head] * score_scale, NEGATIVE)
        weights = jnp.exp(masked - jnp.max(masked, axis=-1, keepdims=True))
        probs.append(weights * (1.0 / jnp.sum(weights, axis=-1, keepdims=True)))
    probs_bf = [p.astype(jnp.bfloat16) for p in probs]
    for head in each_head:
        context[:, at_head[head]] = product(probs_bf[head], values[head]).astype(jnp.bfloat16)
    score_grads = []
    for head in each_head:
        delta = jnp.sum(probs[head] * prob_grads[head], axis=-1, keepdims=True)
        grad = probs[head] * (prob_grads[head] - delta) * score_scale
        score_grads.append(grad.astype(jnp.bfloat16))
    for head in each_head:
        value_grad = transposed_times(probs_bf[head], context_grad[head])
        query_grad = product(score_grads[head], keys[head])
        key_grad = transposed_times(score_grads[head], queries[head])
        grad = jnp.concatenate([query_grad, key_grad], axis=1)
        back = grad * cos - pltpu.roll(grad, 2 * HEAD - ROT // 2, 1) * low
        back = back - pltpu.roll(grad, ROT // 2, 1) * high
        triple_grads[:, at_pair[head]] = back.astype(jnp.bfloat16)
        triple_grads[:, at_value[head]] = value_grad.astype(jnp.bfloat16)
        bias_sums[0:1, at_pair[head]] = jnp.sum(back, axis=0, keepdims=True)
        bias_sums[0:1, at_value[head]] = jnp.sum(value_grad, axis=0, keepdims=True)

    total = product(context[...], output[...]) + feed[...].astype(jnp.float32)
    both[0] = total.astype(both.dtype)
    for place, weight in ((my_half, mine), (other_half, other)):
        back = times_transposed(triple_grads[...], weight[...])
        sums[0:1, place] = jnp.sum(
            back * normed[:, place].astype(jnp.float32), axis=0, keepdims=True
        )
        sums[1:2, place] = jnp.sum(back, axis=0, keepdims=True)
        slope = back * vectors[0:1, place] + slope_part[:, place].astype(jnp.float32)
        both[1, :, place] = slope.astype(both.dtype)


def attention_gradient_kernel(at, *refs):
    acts, upstreams, contexts, triple_grads = (refs[4 * i : 4 * i + 4] for i in range(4))
    small, keep, send, small_out, grads = refs[16:]
    row, cols = contexts[0].shape

    @pl.loop(0, acts[0].shape[1] // TILE)
    def _(step):
        some = pl.ds(pl.multiple_of(step * TILE, TILE), TILE)
        grads[some, : 3 * cols] = summed_product(
            [r[:, some] for r in acts], [r[...] for r in triple_grads]
        )
        grads[some, 3 * cols :] = summed_product(
            [r[:row, some] for r in upstreams], [r[...] for r in contexts]
        )

    part_rows(at, grads, keep, send, 2)
    rounded = small[...].astype(jnp.bfloat16)
    small_out[...] = rounded
    send[keep.shape[0] * keep.shape[1] :] = rounded


def small_kernel(at, upstream, feed_sums, *refs):
    attend_sums, bias_sums, out = refs[:4], refs[4:8], refs[8]
    cols, row = bias_sums[0].shape[1], upstream.shape[0] - 16
    out[...] = jnp.zeros_like(out)
    out[0:2] = sum(ref[0:2] for ref in attend_sums)
    out[2:4] = feed_sums[0:2]
    out[4:5] = jnp.sum(upstream[:row].astype(jnp.float32), axis=0, keepdims=True)
    part = at[0] * 2 + at[1]
    out[pl.ds(5 + part, 1)] = feed_sums[2:3]
    out[pl.ds(9 + part, 1), :cols] = sum(ref[0:1] for ref in bias_sums)


def spread_small(at, small, outs, everywhere):
    *vectors, expand_bias, triple_bias = outs
    half = vectors[0].shape[0]
    units, cols = expand_bias.shape[0] // 2, triple_bias.shape[0] // 6
    for side in range(2):

        @pl.when(at[0] == side)
        def _(side=side):
            for index, vector in enumerate(vectors):
                vector[...] = small[min(index, 4), side * half : (side + 1) * half]
            for core in range(2):
                expand_bias[core * units : (core + 1) * units] = small[5 + side * 2 + core]

    for part in range(4):
        for head in range(cols // HEAD):
            for kind in range(3):
                start = head * 2 * HEAD + kind * HEAD if kind < 2 else 2 * cols + head * HEAD
                to = kind * 4 * cols + part * cols + head * HEAD
                everywhere[:, to : to + HEAD] = small[9 + part : 10 + part, start : start + HEAD]
    mine = pl.ds(pl.multiple_of(at[0] * 6 * cols, 128), 6 * cols)
    triple_bias[...] = everywhere[:, mine].reshape(6 * cols)


def theirs_kernel(at, kept, got, out):
    out[...] = (kept[...] + got[...].astype(jnp.float32)).astype(jnp.bfloat16)


def output_kernel(at, kept, got, got_across, hidden, upstream, vectors, block_out, input_slope):
    inputs = hidden[...].astype(jnp.float32)
    out, slope = (
        kept[i] + got[i].astype(jnp.float32) + got_across[i].astype(jnp.float32) for i in range(2)
    )
    block_out[...] = (inputs + out + vectors[4:5] + vectors[5:6]).astype(jnp.bfloat16)
    normed, scale = normalize(inputs)
    back = norm_back(slope, normed, scale, 1.0)
    input_slope[...] = upstream[: inputs.shape[0]].astype(jnp.float32) + back


def halve_kernel(at, keep, got, *refs, bit):
    *small, own, send = refs[: len(refs) // 2 + 1]
    small_out = refs[len(refs) // 2 + 1 :]
    count, rows = keep.shape[0], keep.shape[1]
    mine = (at[3] >> bit) & 1
    for each in range(count // 2):
        stay, leave = 2 * each + mine, 2 * each + 1 - mine
        theirs = got[pl.ds(pl.multiple_of(stay * rows, 16), rows)]
        own[each] = keep[stay] + theirs.astype(jnp.float32)
        theirs = got[pl.ds(pl.multiple_of(leave * rows, 16), rows)]
        total = keep[leave] + theirs.astype(jnp.float32)
        send[each * rows : (each + 1) * rows] = total.astype(jnp.bfloat16)
    if small:
        both = small[0][...].astype(jnp.float32) + got[count * rows :].astype(jnp.float32)
        both = both.astype(jnp.bfloat16)
        small_out[0][...] = both
        send[count // 2 * rows :] = both


def total_kernel(at, own, got, out):
    out[...] = (own[0] + got[...].astype(jnp.float32)).astype(jnp.bfloat16)


def swap_kernel(at, own, got, small, total, leave):
    rows, columns = total.shape[0] // 2, leave.shape[1] * 3 // 4
    total[...] = (own[0] + got[: 2 * rows].astype(jnp.float32)).astype(jnp.bfloat16)
    leave[:rows, :columns] = total[pl.ds(pl.multiple_of((1 - at[0]) * rows, 16), rows), :columns]
    leave[:rows, columns:] = jnp.zeros((rows, leave.shape[1] - columns), jnp.bfloat16)
    both = small[...].astype(jnp.float32) + got[2 * rows :].astype(jnp.float32)
    leave[rows:] = both.astype(jnp.bfloat16)


def merge_kernel(at, total, leave, got, out, small):
    rows = out.shape[0]
    columns = got.shape[1] * 3 // 4
    rest = total.shape[1] - columns
    for side in range(2):

        @pl.when(at[0] == side)
        def _(side=side):
            out[:, side * columns : (side + 1) * columns] = total[side * rows : (side + 1) * rows, :columns]
            out[:, (1 - side) * columns : (2 - side) * columns] = got[:rows, :columns]

    for side in range(2):
        start = 2 * columns + side * rest
        out[:, start : start + rest] = total[side * rows : (side + 1) * rows, columns:]
    both = leave[rows:].astype(jnp.float32) + got[rows:].astype(jnp.float32)
    small[...] = both.astype(jnp.bfloat16)


def join_kernel(at, *refs):
    *pieces, out = refs
    rows = pieces[0].shape[0]
    for step, piece in enumerate(pieces):
        out[pl.ds(pl.multiple_of((at[3] ^ step) * rows, 16), rows)] = piece[...]


def join_last_kernel(at, *refs):
    *pieces, small, out = refs
    join_kernel(at, *pieces, out)
    rows, width = len(pieces) * pieces[0].shape[0], small.shape[1]
    out[rows:, :width] = small[...]
    out[rows:, width:] = jnp.zeros((16, out.shape[1] - width), jnp.bfloat16)


def finish_rows_kernel(at, own, far, own_other, far_other, out):
    rows = own.shape[0]
    for core, pair in enumerate(((own, far), (own_other, far_other))):
        for side, piece in enumerate(pair):
            start = ((at[1] ^ core) * 2 + (at[2] ^ side)) * rows
            out[pl.ds(pl.multiple_of(start, 16), rows)] = piece[...].astype(jnp.float32)


def finish_columns_kernel(at, own, far, own_other, far_other, out):
    rows, cols = own.shape
    for core, pair in enumerate(((own, far), (own_other, far_other))):
        for side, piece in enumerate(pair):
            at_rows = pl.ds(pl.multiple_of((at[2] ^ side) * rows, 16), rows)
            at_cols = pl.ds(pl.multiple_of((at[1] ^ core) * cols, 128), cols)
            out[at_rows, at_cols] = piece[...].astype(jnp.float32)


def spread_columns(at, own, other, out):
    rows, cols = out.shape[0], out.shape[1] // 12

    def place(source, core):
        for side in range(2):
            part, base = side * 2 + core, side * 3 * cols
            for head in range(cols // HEAD):
                for kind in range(3):
                    start = head * 2 * HEAD + kind * HEAD if kind < 2 else 2 * cols + head * HEAD
                    to = kind * 4 * cols + part * cols + head * HEAD
                    piece = source[:rows, base + start : base + start + HEAD]
                    out[:, to : to + HEAD] = piece.astype(jnp.float32)

    for core in range(2):

        @pl.when(at[1] == core)
        def _(core=core):
            place(own, core)
            place(other, 1 - core)


def first_half_kernel(at, own, own_other, triple, held, sem):
    spread_columns(at, own, own_other, held)
    rows = held.shape[0]
    mine = pl.ds(pl.multiple_of(at[2] * rows, 8), rows)
    copy = pltpu.make_async_copy(held, triple.at[mine], sem)
    copy.start()
    copy.wait()


def finish_attention_kernel(at, own, far, own_other, far_other, _, *refs):
    triple, output, *vectors = refs[:10]
    mine, other, small, everywhere, held, sem = refs[10:]
    rows, half = own.shape[0], mine.shape[0]
    cols = output.shape[0] // 2
    spread_columns(at, far, far_other, held)
    theirs = pl.ds(pl.multiple_of((1 - at[2]) * rows, 8), rows)
    copy = pltpu.make_async_copy(held, triple.at[theirs], sem)
    copy.start()
    turned = slice(6 * cols, 8 * cols)
    for target, pair in ((mine, (own, far)), (other, (own_other, far_other))):
        for side, piece in enumerate(pair):
            at_rows = pl.ds(pl.multiple_of((at[2] ^ side) * rows, 16), rows)
            target[at_rows] = piece[:rows, turned].astype(jnp.float32)
    for index, source in enumerate((mine, other)):
        at_core = pl.ds(pl.multiple_of((at[1] ^ index) * cols, 64), cols)
        for side in range(2):
            columns = slice(side * half, (side + 1) * half)
            output[at_core, columns] = source[:, side * cols : (side + 1) * cols].T
    small[...] = far[rows:, : small.shape[1]].astype(jnp.float32) + far_other[
        rows:, : small.shape[1]
    ].astype(jnp.float32)
    spread_small(at, small, vectors, everywhere)
    copy.wait()


def split_body(groups):
    depth = groups // 4

    def flip_dp(values, bits):
        return lax.ppermute(values, "dp", [(i, i ^ bits) for i in range(groups)])

    def flip_core(values):
        return flip_dp(values, 1)

    def flip_y(values):
        return flip_dp(values, 2)

    def flip_x(values):
        return lax.ppermute(values, "shard", [(0, 1), (1, 0)])

    def body(
        hidden_in,
        cotangent,
        segment_ids,
        live_mask,
        attend_gain,
        attend_shift,
        feed_gain,
        feed_shift,
        triple_weight,
        triple_bias,
        output_weight,
        output_bias,
        expand_weight,
        expand_bias,
        reduce_weight,
        reduce_bias,
    ):
        return layer(
            hidden_in, cotangent, segment_ids, live_mask,
            (attend_gain, attend_shift, feed_gain, feed_shift, output_bias, reduce_bias),
            triple_weight, triple_bias, output_weight, expand_weight, expand_bias, reduce_weight,
        )

    def layer(
        hidden_in, cotangent, segment_ids, live_mask, six_vectors,
        triple_weight, triple_bias, output_weight, expand_weight, expand_bias, reduce_weight,
    ):
        row, width = hidden_in.shape
        tokens = 4 * row
        side = lax.axis_index("shard")
        place = lax.axis_index("dp")
        core = place & 1
        at = jnp.stack([side, core, (place >> 1) & 1, place >> 2]).astype(jnp.int32)
        cols = triple_weight.shape[1] // 12
        units = expand_weight.shape[1] // 2
        half = width // 2
        f32 = jnp.float32

        def gather_rows(values):
            across = flip_x(values)
            return (values, flip_core(values), across, flip_core(across))

        given = (*six_vectors, triple_bias, expand_bias, cotangent, segment_ids, live_mask)
        packed, expand_bias_mine, upstream_own = local_call(
            first_kernel,
            [
                shape_of(16, half, dtype=f32),
                shape_of(8, units, dtype=f32),
                shape_of(row + 16, width),
            ],
            (at, *given),
            [pltpu.VMEM(a.shape, a.dtype) for a in given]
            + [pltpu.SemaphoreType.DMA((len(given),))],
            room=62,
            space=pltpu.HBM,
        )
        packed_other = flip_x(packed)
        hidden = gather_rows(hidden_in)
        upstreams = gather_rows(upstream_own)
        _, full, bias = local_call(
            vectors_kernel,
            [
                shape_of(1, 12 * cols, dtype=f32),
                shape_of(6, width, dtype=f32),
                shape_of(1, 3 * cols, dtype=f32),
            ],
            (at, packed, packed_other),
        )
        freqs = 10000.0 ** (-np.arange(0, ROT, 2, dtype=np.float32) / ROT)
        freqs = jnp.asarray(np.broadcast_to(freqs[:, None], (ROT // 2, 128)).astype(np.float32))
        triple_mine, triple_send, expand_mine, reduce_mine, output_mine = local_call(
            weights_kernel,
            [
                shape_of(half, 3 * cols),
                shape_of(half, 3 * cols),
                shape_of(width, units),
                shape_of(units, width),
                shape_of(cols, width),
            ],
            (at, triple_weight, expand_weight, reduce_weight, output_weight),
            [pltpu.VMEM(triple_weight.shape, jnp.bfloat16), pltpu.SemaphoreType.DMA((4,))],
            room=46,
            space=pltpu.HBM,
        )
        triple_other = flip_x(triple_send)
        piece_rows = half // depth
        keep_shape = shape_of(depth, piece_rows, width, dtype=f32)
        send_shape = shape_of(half, width)
        flops = 2 * tokens * width * units
        tiles = []
        for index in range(2):
            outs = local_call(
                feed_forward_kernel,
                [shape_of(row, width)] * 12,
                (
                    at, *hidden[2 * index : 2 * index + 2], full, expand_mine,
                    expand_bias_mine, reduce_mine,
                ),
                flops=flops,
            )
            tiles += [outs[:6], outs[6:]]
        act_ones, act_twos, normeds, feeds, slopes, feed_hiddens = zip(*tiles)
        reduce_parts = local_call(
            reduce_gradient_kernel,
            [keep_shape, send_shape],
            (at, *feed_hiddens, *upstreams),
            [pltpu.VMEM((units, width), f32)],
            flops,
        )
        *slope_parts, feed_sums, keep, send = local_call(
            feed_backward_kernel,
            [shape_of(row, width)] * 4 + [shape_of(8, width, dtype=f32), keep_shape, send_shape],
            (at, *act_twos, *upstreams, *normeds, *slopes, full, expand_mine, reduce_mine),
            [pltpu.VMEM((tokens, units), jnp.bfloat16), pltpu.VMEM((width, units), f32)],
            3 * flops,
        )
        expand_parts = keep, send
        attended = [None] * 4
        for index in (1, 3, 0, 2):
            kind = jnp.bfloat16 if index % 2 else f32
            attended[index] = local_call(
                attention_kernel,
                [
                    shape_of(2, row, width, dtype=kind),
                    shape_of(row, cols),
                    shape_of(row, 3 * cols),
                    shape_of(8, width, dtype=f32),
                    shape_of(8, 3 * cols, dtype=f32),
                ],
                (
                    at, freqs, act_ones[index], upstreams[index], normeds[index],
                    feeds[index], slope_parts[index], full, triple_mine, triple_other, bias,
                    output_mine,
                ),
                flops=flops,
            )
        boths, contexts, triple_grads, attend_sums, bias_sums = zip(*attended)
        (small,) = local_call(
            small_kernel,
            [shape_of(16, width, dtype=f32)],
            (at, upstream_own, feed_sums, *attend_sums, *bias_sums),
            room=2,
        )
        triple_parts = local_call(
            attention_gradient_kernel,
            [keep_shape, shape_of(half + 16, width), shape_of(16, width)],
            (at, *act_ones, *upstreams, *contexts, *triple_grads, small),
            [pltpu.VMEM((width, 4 * cols), f32)],
            flops,
        )

        (theirs,) = local_call(
            theirs_kernel, [shape_of(2, row, width)], (at, boths[2], flip_core(boths[3])), room=2
        )
        block_out, input_slope = local_call(
            output_kernel,
            [shape_of(row, width), shape_of(row, width, dtype=f32)],
            (
                at, boths[0], flip_core(boths[1]), flip_x(theirs), hidden_in,
                upstream_own, full,
            ),
            room=6,
        )

        def reduce_pieces(keep, send, *small):
            got, count, extra = flip_y(send), depth, 16 * len(small)
            for bit in range(depth.bit_length() - 1):
                count //= 2
                keep, send, *small = local_call(
                    functools.partial(halve_kernel, bit=bit),
                    [
                        shape_of(count, piece_rows, width, dtype=f32),
                        shape_of(count * piece_rows + extra, width),
                    ]
                    + [shape_of(16, width)] * len(small),
                    (at, keep, got, *small),
                    room=2,
                )
                got = flip_dp(send, 4 << bit)
            piece = shape_of(piece_rows, width)
            if not small:
                return local_call(total_kernel, [piece], (at, keep, got), room=2)
            rows = piece_rows // 2
            total, leave = local_call(
                swap_kernel, [piece, shape_of(rows + 16, width)], (at, keep, got, *small), room=2
            )
            return local_call(
                merge_kernel,
                [shape_of(rows, 2 * width), shape_of(16, width)],
                (at, total, leave, flip_x(leave)),
                room=2,
            )

        def gather_pieces(piece, *more):
            pieces, step = [piece] + [None] * (depth - 1), depth
            while step > 1:
                step //= 2
                for at_piece in range(step, depth, 2 * step):
                    near = pieces[at_piece - step]
                    pieces[at_piece] = flip_dp(near, 4 * step)
            rows, cols = depth * piece.shape[0], piece.shape[1]
            (own,) = local_call(join_kernel, [shape_of(rows, cols)], (at, *pieces), room=2)
            own_other = flip_core(own)
            far = [flip_y(each) for each in pieces]
            (far,) = local_call(
                join_last_kernel if more else join_kernel,
                [shape_of(rows + 16 * len(more), cols)],
                (at, *far, *more),
                room=2,
            )
            return at, own, far, own_other, flip_core(far)

        (reduce_sum,) = local_call(
            finish_rows_kernel,
            [shape_of(2 * units, width, dtype=f32)],
            gather_pieces(*reduce_pieces(*reduce_parts)),
            room=2,
        )
        (expand_sum,) = local_call(
            finish_columns_kernel,
            [shape_of(width, 2 * units, dtype=f32)],
            gather_pieces(*reduce_pieces(*expand_parts)),
            room=2,
        )
        vector = shape_of(half, dtype=f32)
        _, own, far, own_other, far_other = gather_pieces(*reduce_pieces(*triple_parts))
        triple_shape = shape_of(half, 12 * cols, dtype=f32)
        held = pltpu.VMEM((half // 2, 12 * cols), f32)
        (triple_first,) = local_call(
            first_half_kernel,
            [triple_shape],
            (at, own, own_other),
            [held, pltpu.SemaphoreType.DMA(())],
            room=2,
            hbm_out=True,
        )
        triple_sum, output_sum, *vectors, bias_sum, bias_again, expand_bias_sum, triple_bias_sum = (
            local_call(
                finish_attention_kernel,
                [triple_shape, shape_of(2 * cols, width, dtype=f32)]
                + [vector] * 6
                + [shape_of(2 * units, dtype=f32), shape_of(6 * cols, dtype=f32)],
                (at, own, far, own_other, far_other, triple_first),
                [
                    pltpu.VMEM((half, 2 * cols), f32),
                    pltpu.VMEM((half, 2 * cols), f32),
                    pltpu.VMEM((16, width), f32),
                    pltpu.VMEM((1, 12 * cols), f32),
                    held,
                    pltpu.SemaphoreType.DMA(()),
                ],
                room=4,
                hbm_out=True,
                alias=5,
            )
        )
        return (
            block_out,
            input_slope,
            *vectors,
            triple_sum,
            triple_bias_sum,
            output_sum,
            bias_sum,
            expand_sum,
            expand_bias_sum,
            reduce_sum,
            bias_again,
        )

    return body


def solution(mesh):
    placed = (
        P(("dp", "shard"), None),
        P(("dp", "shard"), None),
        P(("dp", "shard")),
        P(("dp", "shard")),
        P("shard"),
        P("shard"),
        P("shard"),
        P("shard"),
        P("shard", None),
        P("shard"),
        P("shard", None),
        P("shard"),
        P(None, "shard"),
        P("shard"),
        P("shard", None),
        P("shard"),
    )
    split = mesh.shape['shard'] == 2 and HEADS % 4 == 0
    whole_rows = mesh.shape['dp'] >= 8 and mesh.shape['dp'] & (mesh.shape['dp'] - 1) == 0
    split = split and whole_rows
    body = split_body(mesh.shape['dp']) if split else gathered_body
    return jax.shard_map(
        body,
        mesh=mesh,
        in_specs=placed,
        out_specs=(
            P(("dp", "shard"), None),
            P(("dp", "shard"), None),
            P("shard"),
            P("shard"),
            P("shard"),
            P("shard"),
            P("shard", None),
            P("shard"),
            P("shard", None),
            P("shard"),
            P(None, "shard"),
            P("shard"),
            P("shard", None),
            P("shard"),
        ),
        check_vma=False,
    )
```
